512 devices in a mesh: pert: 16 (over x_lo, y), doc: 32 (over x_hi, z, core).
Axes of the slice: x: 4 (x_hi: 2, x_lo: 2; x = x_hi * 2 + x_lo), y: 8, z: 8, core: 2. Of those that a mesh axis runs over, the one named last changes fastest.
Arguments:
- counts: int32 [16, 256, 16384], P('pert', 'doc'), may hold values from 1 to 11
- tile_mask: int32 [16, 256, 128], P('pert', 'doc'), may hold values 0 or 1
- member_topics: float32 [16, 256, 64], P('pert', 'doc'), may hold values from 0.05 to 0.5
- start_dict: float32 [16, 16384, 64], P('pert', 'doc'), may hold values from 0.05 to 0.5
- align_perm: int32 [16, 64], P('pert'), may hold values from 0 to 63, each once within a row
- base_counts: int32 [2048, 16384], P(('pert', 'doc')), may hold values from 1 to 11
- base_topics: float32 [2048, 64], P(('pert', 'doc')), may hold values from 0.05 to 0.5
Outputs:
- median_dict: float32 [32, 16, 32, 64], P('doc', 'pert')
- refit_topics: float32 [2048, 64], P(('pert', 'doc'))
The draws below stay inside these ranges and needn't reach their ends.
Inputs may be any that keep to these rules, and one draw needn't show every extreme that they name: `align_perm`: each row is a permutation of 0 to 63.
All inputs are finite; a program needn't handle non-finite values. No bound on the sum of `tile_mask` on one device may be relied on, other than what follows from the above.
Results may differ from the reference program's by a relative error of at most 0.0003.
Values sent between devices are 32-bit elements; how exact they have to be, the bound alone decides.
A program may use at most 64 MiB of HBM per device.

```python
import math
import jax
import jax.numpy as jnp
from jax import lax

WORDS = 16384
K = 64
ODOC_DEV = 4
UPDATES = 3
REFITS = 2
MEMBERS = 16
MDOCS = 256
ODOCS = 2048
WTILES = 128
SUB = 32
N_PERT = 16
N_DOC = 32


def with_ends(array, rng, low, high):
    longest = array.shape.index(max(array.shape))
    spots = []
    for shift in (0, 1):
        where = [jax.random.randint(jax.random.fold_in(rng, axis), (), 0, length) for axis, length in enumerate(array.shape)]
        where[longest] = (where[longest] + shift) % array.shape[longest]
        spots.append(tuple(where))
    return array.at[spots[0]].set(low).at[spots[1]].set(high)


def block_levels(rng, dims, shards, least, high):
    factor_of, own = 1.0, jax.random.fold_in(rng, 6)
    for axis_at, parts in shards:
        heights = jnp.exp(jax.random.uniform(jax.random.fold_in(own, axis_at), (parts,), jnp.float32, least / len(shards), high / len(shards)))
        factor_of = factor_of * jnp.repeat(heights, dims[axis_at] // parts).reshape([-1 if axis == axis_at else 1 for axis in range(len(dims))])
    return factor_of


def setup_inputs(seed: int = 0) -> dict:
    streams_of = jax.random.split(jax.random.key(seed), 8)
    return {
        "counts": with_ends(jax.random.randint(streams_of[0], (MEMBERS, MDOCS, WORDS), 1, 12), jax.random.fold_in(streams_of[0], 1), 1, 11).astype(jnp.int32),
        "tile_mask": with_ends((jax.random.randint(streams_of[1], (MEMBERS, MDOCS, WTILES), 0, 2) < 1).astype(jnp.int32), jax.random.fold_in(streams_of[1], 1), 0, 1),
        "member_topics": jnp.clip(jnp.exp(math.log(0.5) - 2.3025851 * jax.random.uniform(streams_of[2], (MEMBERS, MDOCS, K), jnp.float32) ** block_levels(streams_of[2], (MEMBERS, MDOCS, K), ((0, 16), (1, 32)), -0.2, 0.2)), 0.05, 0.5),
        "start_dict": jnp.clip(jnp.exp(math.log(0.5) - 2.3025851 * jax.random.uniform(streams_of[3], (MEMBERS, WORDS, K), jnp.float32) ** block_levels(streams_of[3], (MEMBERS, WORDS, K), ((0, 16), (1, 32)), -0.2, 0.2)), 0.05, 0.5),
        "align_perm": jax.vmap(lambda own: jax.random.permutation(own, K))(jax.random.split(streams_of[4], MEMBERS)).reshape((MEMBERS, K)).astype(jnp.int32),
        "base_counts": with_ends(jax.random.randint(streams_of[5], (ODOCS, WORDS), 1, 12), jax.random.fold_in(streams_of[5], 1), 1, 11).astype(jnp.int32),
        "base_topics": jnp.clip(jnp.exp(math.log(0.5) - 2.3025851 * jax.random.uniform(streams_of[6], (ODOCS, K), jnp.float32) ** block_levels(streams_of[6], (ODOCS, K), ((0, 512),), -0.2, 0.2)), 0.05, 0.5),
    }


HIGHEST_PRECISION = lax.Precision.HIGHEST


def product_t(left_side, right_side):
    return lax.dot_general(left_side, right_side, (((1,), (1,)), ((), ())), precision=HIGHEST_PRECISION)


def weight_update(topics, quotient, dictionary, col_total):
    return topics * jnp.dot(quotient, dictionary, precision=HIGHEST_PRECISION) / col_total


def middle(stacked):
    ordered = jnp.sort(stacked, axis=0)
    middle_at = stacked.shape[0] // 2
    return 0.5 * (ordered[middle_at - 1] + ordered[middle_at])


def occupied_counts(counts, mask, first_doc):
    doc_count, word_count = counts.shape
    tile_count = mask.shape[1]
    tile_width = word_count // tile_count
    tile_ids = lax.broadcasted_iota(jnp.int32, (doc_count, tile_count), 1)
    doc_ids = first_doc + lax.broadcasted_iota(jnp.int32, (doc_count, tile_count), 0)
    occupied = jnp.maximum(mask, (tile_ids == doc_ids % tile_count).astype(jnp.int32)).astype(jnp.float32)
    spread = counts.astype(jnp.float32).reshape(doc_count, tile_count, tile_width) * occupied[:, :, None]
    return spread.reshape(doc_count, word_count)


def reference(counts, tile_mask, member_topics, start_dict, align_perm, base_counts, base_topics):
    def one_member(inputs):
        counts_m, mask_m, topics, dictionary, perm_m = inputs
        weighted = occupied_counts(counts_m, mask_m, 0)
        col_total = jnp.sum(dictionary, axis=0)
        for iteration in range(UPDATES):
            quotient = weighted / product_t(topics, dictionary)
            topics = weight_update(topics, quotient, dictionary, col_total)
        quotient = weighted / product_t(topics, dictionary)
        numerator = lax.dot_general(quotient, topics, (((0,), (0,)), ((), ())), precision=HIGHEST_PRECISION)
        topic_load = jnp.sum(topics, axis=0)
        new_dict = dictionary * numerator / topic_load
        return jnp.take(new_dict, perm_m.astype(jnp.int32), axis=1)

    aligned = lax.map(one_member, (counts, tile_mask, member_topics, start_dict, align_perm))
    median = middle(aligned)
    median_total = jnp.sum(median, axis=0)

    def refit_block(inputs):
        counts_b, topics_b = inputs
        weighted = counts_b.astype(jnp.float32)
        for iteration in range(REFITS):
            quotient = weighted / product_t(topics_b, median)
            topics_b = weight_update(topics_b, quotient, median, median_total)
        return topics_b

    blocks = N_PERT * N_DOC
    refit = lax.map(refit_block, (base_counts.reshape(blocks, ODOC_DEV, WORDS), base_topics.reshape(blocks, ODOC_DEV, K)))
    return median.reshape(N_DOC, N_PERT, SUB, K), refit.reshape(ODOCS, K)
```

```python
import functools

import jax
import jax.numpy as jnp
from jax import lax
from jax.experimental import pallas as pl
from jax.experimental.pallas import tpu as pltpu
from jax.sharding import PartitionSpec as P

UPDATES = 3
REFITS = 2
NX = 2
NC = 2
NW = NX * NC
MESH = pl.DeviceIdType.MESH
F32 = jnp.float32
BF16 = jnp.bfloat16


def sort_pairs(count):
    pairs = []
    span = 1
    while span < count:
        step = span
        while step >= 1:
            for start in range(step % span, count - step, 2 * step):
                for at in range(min(step, count - start - step)):
                    low, high = start + at, start + at + step
                    if low // (2 * span) == high // (2 * span):
                        pairs.append((low, high))
            step //= 2
        span *= 2
    return pairs


def middle(rows):
    rows = list(rows)
    for low, high in sort_pairs(len(rows)):
        rows[low], rows[high] = jnp.minimum(rows[low], rows[high]), jnp.maximum(rows[low], rows[high])
    at = len(rows) // 2
    return 0.5 * (rows[at - 1] + rows[at])


def split2(x):
    high = x.astype(BF16)
    return high, (x - high.astype(F32)).astype(BF16)


def split3(x):
    high = x.astype(BF16)
    rest = x - high.astype(F32)
    mid = rest.astype(BF16)
    return high, mid, (rest - mid.astype(F32)).astype(BF16)


def pack(x):
    half = x.shape[0] // 2
    return jnp.concatenate([x[:half], x[half:]], axis=1)


def unpack(x):
    half = x.shape[1] // 2
    return jnp.concatenate([x[:, :half], x[:, half:]], axis=0)


def turn_tall(x):
    wide = jnp.concatenate([x, jnp.zeros_like(x)], axis=1)
    return wide.T[: x.shape[1]]


def turn_flat(x):
    tall = jnp.concatenate([x, jnp.zeros_like(x)], axis=0)
    return tall.T[:, : x.shape[0]]


def dot(a, b):
    return jnp.dot(a, b, preferred_element_type=F32)


def dot_nt(a, b):
    return lax.dot_general(a, b, (((1,), (1,)), ((), ())), preferred_element_type=F32)


def kernel(
    counts_ref, mask_ref, mtop_ref, dict_ref, perm_ref, base_ref, btop_ref,
    med_ref, refit_ref,
    masked, data4, data32, bsend, base4, mtop4, btop4, dgather, mgather, dsplit, msplit,
    mpartial, bpartial, topics_z, q3, p2_send, p2_recv, p3_recv,
    w_send, w_recv, b_send, b_recv, t_send, t_recv, u_send, u_recv, rd_send, rd_recv, rm_send, rm_recv,
    a_send, a_recv, z_send, z_recv, g_send, g_recv, s_send, s_recv, m_send, m_recv,
    *, np_, nz,
):
    wb, k = dict_ref.shape
    docs, bdocs = mtop_ref.shape[0], btop_ref.shape[0]
    p = lax.axis_index("pert")
    b = lax.axis_index("doc")
    xh, z, c = b // (nz * NC), (b // NC) % nz, b % NC
    w = xh * NC + c
    chunk = k // 2
    slab = wb // np_

    def w_device(at):
        return (p, (at // NC) * (nz * NC) + z * NC + at % NC)

    def z_device(at):
        return (p, xh * (nz * NC) + at * NC + c)

    def p_device(at):
        return (at, b)

    w_peers = [lax.rem(w + i, NW) for i in range(1, NW)]
    z_peers = [lax.rem(z + i, nz) for i in range(1, nz)]
    p_peers = [lax.rem(p + i, np_) for i in range(1, np_)]

    barrier = pltpu.get_barrier_semaphore()
    for peer in w_peers:
        pl.semaphore_signal(barrier, inc=1, device_id=w_device(peer), device_id_type=MESH)
    for peer in z_peers:
        pl.semaphore_signal(barrier, inc=1, device_id=z_device(peer), device_id_type=MESH)
    for peer in p_peers:
        pl.semaphore_signal(barrier, inc=1, device_id=p_device(peer), device_id_type=MESH)

    tiles = mask_ref.shape[1]
    tile_width = counts_ref.shape[1] // tiles
    per_block = wb // tile_width
    tile_ids = lax.broadcasted_iota(jnp.int32, (docs, tiles), 1)
    doc_ids = b * docs + lax.broadcasted_iota(jnp.int32, (docs, tiles), 0)
    occupied = jnp.maximum(mask_ref[...], (tile_ids == doc_ids % tiles).astype(jnp.int32)).astype(F32)

    for owner in range(NW):

        def mask_block(zb, carry, owner=owner):
            block = ((owner // NC) * nz + zb) * NC + owner % NC
            for j in range(per_block):
                tile = block * per_block + j
                seen = jnp.sum(jnp.where(tile_ids == tile, occupied, 0.0), axis=1, keepdims=True)
                at = pl.multiple_of(tile * tile_width, tile_width)
                masked[owner, zb, :, j * tile_width : (j + 1) * tile_width] = (
                    counts_ref[:, pl.ds(at, tile_width)].astype(F32) * seen
                )
            at = pl.multiple_of(block * wb, wb)
            bsend[owner, zb] = base_ref[:, pl.ds(at, wb)].astype(F32)
            return carry

        lax.fori_loop(0, nz, mask_block, 0)
    dgather[z] = turn_tall(dict_ref[...])

    pl.semaphore_wait(barrier, NW - 1 + nz - 1 + np_ - 1)

    sends = []

    def remote(src, dst, ssem, rsem, device):
        return pltpu.make_async_remote_copy(
            src_ref=src, dst_ref=dst, send_sem=ssem, recv_sem=rsem, device_id=device, device_id_type=MESH
        )

    def start(copy):
        copy.start()
        sends.append(copy)

    right, left = lax.rem(z + 1, nz), lax.rem(z + nz - 1, nz)
    last = nz // 2

    def ring_block(way, s):
        return lax.rem(z + nz - s, nz) if way == 0 else lax.rem(z + s, nz)

    def ring_chunks(way, s):
        return (0, 1) if s < last else (way,)

    def ring_copy(buf, ssem, rsem, way, s, ch):
        at = buf.at[ring_block(way, s), pl.ds(ch * chunk, chunk), :]
        return remote(at, at, ssem.at[way, s, ch], rsem.at[way, s, ch], z_device(right if way == 0 else left))

    def ring_first(buf, ssem, rsem):
        for ch in (0, 1):
            for way in (0, 1):
                if ch in ring_chunks(way, 1):
                    start(ring_copy(buf, ssem, rsem, way, 0, ch))

    def ring_step(buf, ssem, rsem, s):
        for ch in (0, 1):
            for way in (0, 1):
                if ch in ring_chunks(way, s):
                    here = buf.at[ring_block(way, s), pl.ds(ch * chunk, chunk), :]
                    remote(
                        here, here, ssem.at[way, s - 1, ch], rsem.at[way, s - 1, ch],
                        z_device(right if way == 0 else left),
                    ).wait_recv()
                    if s < last and ch in ring_chunks(way, s + 1):
                        start(ring_copy(buf, ssem, rsem, way, s, ch))

    def blocks_at(s):
        if s == 0 or s == last:
            return [ring_block(0, s)]
        return [ring_block(0, s), ring_block(1, s)]

    def split_block(buf, out, at):
        high, low = split2(buf[at])
        out[at, 0:k] = high
        out[at, k : 2 * k] = low
        out[at, 2 * k : 3 * k] = high

    def stack_topics(topics):
        high, low = split2(topics)
        return jnp.concatenate([high, high, low], axis=1)

    def rows_of(buf, at):
        return jnp.concatenate([buf[owner, at] for owner in range(NW)], axis=0)

    def block_term(stacked, buf, split, at):
        data = rows_of(buf, at)
        rows = data.shape[0]
        high, low = split2(data / dot(stacked, split[at]))
        both = dot_nt(jnp.concatenate([high, low], axis=0), split[at, 0 : 2 * k])
        return both[:rows] + both[rows:]

    def column_term(split, at):
        return dot_nt(jnp.ones((16, wb), BF16), split[at, 0 : 2 * k])[:8]

    def fold(x):
        return x[:, :k] + x[:, k:]

    def all_terms(stacked, buf, split):
        def one(at, acc):
            return acc + block_term(stacked, buf, split, at)

        return lax.fori_loop(0, nz, one, jnp.zeros((stacked.shape[0], 2 * k), F32))

    def exchange(partial, at, number, acc, columns):
        rows = acc.shape[0] // 2
        partial[at, w, 0:rows] = pack(fold(acc))
        sent = rows
        if columns is not None:
            partial[at, w, rows : rows + 8] = columns
            sent = rows + 8
        for i, peer in enumerate(w_peers):
            mine = partial.at[at, w, 0:sent]
            start(remote(mine, mine, a_send.at[number, i], a_recv.at[number, w], w_device(peer)))
        for i, peer in enumerate(w_peers):
            theirs = partial.at[at, peer, 0:sent]
            remote(theirs, theirs, a_send.at[number, i], a_recv.at[number, peer], w_device(peer)).wait_recv()
        total = partial[at, 0, 0:sent]
        for owner in range(1, NW):
            total = total + partial[at, owner, 0:sent]
        product = unpack(total[:rows])
        return product, (fold(total[rows : rows + 1]) if columns is not None else None)

    ring_first(dgather, rd_send, rd_recv)
    for i, peer in enumerate(w_peers):
        start(remote(mtop_ref, mtop4.at[w], t_send.at[i], t_recv.at[w], w_device(peer)))
        start(remote(btop_ref, btop4.at[w], u_send.at[i], u_recv.at[w], w_device(peer)))
        start(remote(masked.at[peer], data4.at[w], w_send.at[i], w_recv.at[w], w_device(peer)))
    data4[w] = masked[w]
    base4[w] = bsend[w]
    mtop4[w] = mtop_ref[...]
    btop4[w] = btop_ref[...]
    split_block(dgather, dsplit, z)

    columns = column_term(dsplit, z)
    for s in range(1, last):
        ring_step(dgather, rd_send, rd_recv, s)
        for at in blocks_at(s):
            split_block(dgather, dsplit, at)
            columns = columns + column_term(dsplit, at)
    for i, peer in enumerate(w_peers):
        remote(mtop_ref, mtop4.at[peer], t_send.at[i], t_recv.at[peer], w_device(peer)).wait_recv()
        remote(btop_ref, btop4.at[peer], u_send.at[i], u_recv.at[peer], w_device(peer)).wait_recv()
        remote(masked.at[peer], data4.at[peer], w_send.at[i], w_recv.at[peer], w_device(peer)).wait_recv()
    topics = jnp.concatenate([mtop4[owner] for owner in range(NW)], axis=0)
    stacked = stack_topics(topics)
    acc = jnp.zeros((topics.shape[0], 2 * k), F32)
    for s in range(last):
        for at in blocks_at(s):
            acc = acc + block_term(stacked, data4, dsplit, at)
    ring_step(dgather, rd_send, rd_recv, last)
    for at in blocks_at(last):
        split_block(dgather, dsplit, at)
        columns = columns + column_term(dsplit, at)
        acc = acc + block_term(stacked, data4, dsplit, at)
    product, col_total = exchange(mpartial, 0, 0, acc, columns)
    topics = topics * product / col_total
    for i, peer in enumerate(z_peers):
        start(remote(data4.at[:, peer], data32.at[z], z_send.at[i], z_recv.at[z], z_device(peer)))
    data32[z] = data4[:, z]
    for update in range(1, UPDATES):
        acc = all_terms(stack_topics(topics), data4, dsplit)
        product, _ = exchange(mpartial, update, update, acc, None)
        topics = topics * product / col_total

    topics_z[z] = pack(topics)
    for i, peer in enumerate(z_peers):
        start(remote(topics_z.at[z], topics_z.at[z], g_send.at[i], g_recv.at[z], z_device(peer)))
    for i, peer in enumerate(w_peers):
        start(remote(bsend.at[peer], base4.at[w], b_send.at[i], b_recv.at[w], w_device(peer)))
    for i, peer in enumerate(z_peers):
        remote(data4.at[:, peer], data32.at[peer], z_send.at[i], z_recv.at[peer], z_device(peer)).wait_recv()
    for i, peer in enumerate(z_peers):
        remote(topics_z.at[z], topics_z.at[peer], g_send.at[i], g_recv.at[peer], z_device(peer)).wait_recv()
    rows = NW * docs
    every = jnp.concatenate([unpack(topics_z[at]) for at in range(nz)], axis=0)

    for at in range(nz):
        recon = dot(stack_topics(every[at * rows : (at + 1) * rows]), dsplit[z])
        data = jnp.concatenate([data32[at, owner] for owner in range(NW)], axis=0)
        high, low = split2(data / recon)
        for part, piece in enumerate((high, low, high)):
            q3[(part * nz + at) * rows : (part * nz + at + 1) * rows] = piece
    wide = turn_tall(every)
    high, low = split2(wide)
    numerator = dot(jnp.concatenate([high, high, low], axis=1), q3[...])
    new_dict = dgather[z] * numerator / jnp.sum(wide, axis=1, keepdims=True)

    onehot = (lax.broadcasted_iota(jnp.int32, (k, k), 0) == perm_ref[...]).astype(F32).astype(BF16)
    aligned = dot(
        jnp.concatenate(split3(turn_flat(new_dict)), axis=1), jnp.concatenate([onehot, onehot, onehot], axis=0)
    )
    for at in range(np_):
        p2_send[at] = pack(aligned[at * slab : (at + 1) * slab])
    for i, peer in enumerate(p_peers):
        start(remote(p2_send.at[peer], p2_recv.at[p], s_send.at[i], s_recv.at[p], p_device(peer)))
    p2_recv[p] = p2_send[p]
    for i, peer in enumerate(p_peers):
        remote(p2_send.at[peer], p2_recv.at[peer], s_send.at[i], s_recv.at[peer], p_device(peer)).wait_recv()
    median = middle([p2_recv[at] for at in range(np_)])
    p3_recv[p] = median
    for i, peer in enumerate(p_peers):
        start(remote(p3_recv.at[p], p3_recv.at[p], m_send.at[i], m_recv.at[p], p_device(peer)))
    med_ref[...] = unpack(median)
    for i, peer in enumerate(p_peers):
        remote(p3_recv.at[p], p3_recv.at[peer], m_send.at[i], m_recv.at[peer], p_device(peer)).wait_recv()

    mgather[z] = turn_tall(jnp.concatenate([unpack(p3_recv[at]) for at in range(np_)], axis=0))
    ring_first(mgather, rm_send, rm_recv)
    for i, peer in enumerate(w_peers):
        remote(bsend.at[peer], base4.at[peer], b_send.at[i], b_recv.at[peer], w_device(peer)).wait_recv()
    topics = jnp.concatenate([btop4[owner] for owner in range(NW)], axis=0)
    stacked = stack_topics(topics)
    acc = jnp.zeros((topics.shape[0], 2 * k), F32)
    columns = jnp.zeros((8, 2 * k), F32)
    for s in range(last + 1):
        if s < last:
            ring_step(mgather, rm_send, rm_recv, s + 1)
        for at in blocks_at(s):
            split_block(mgather, msplit, at)
            columns = columns + column_term(msplit, at)
            acc = acc + block_term(stacked, base4, msplit, at)
    product, col_total = exchange(bpartial, 0, UPDATES, acc, columns)
    topics = topics * product / col_total
    for update in range(1, REFITS):
        acc = all_terms(stack_topics(topics), base4, msplit)
        product, _ = exchange(bpartial, update, UPDATES + update, acc, None)
        topics = topics * product / col_total
    own = topics[0:bdocs]
    for owner in range(1, NW):
        own = jnp.where(w == owner, topics[owner * bdocs : (owner + 1) * bdocs], own)
    refit_ref[...] = own

    for copy in sends:
        copy.wait_send()


def per_device(counts, tile_mask, member_topics, start_dict, align_perm, base_counts, base_topics, *, np_, nz):
    docs, bdocs = counts.shape[1], base_counts.shape[0]
    wb, k = start_dict.shape[1:]
    slab = wb // np_
    last = nz // 2
    rows, brows = NW * docs, NW * bdocs
    sem = pltpu.SemaphoreType.DMA
    scratch = [
        pltpu.VMEM((NW, nz, docs, wb), F32),
        pltpu.VMEM((NW, nz, docs, wb), F32),
        pltpu.VMEM((nz, NW, docs, wb), F32),
        pltpu.VMEM((NW, nz, bdocs, wb), F32),
        pltpu.VMEM((NW, nz, bdocs, wb), F32),
        pltpu.VMEM((NW, docs, k), F32),
        pltpu.VMEM((NW, bdocs, k), F32),
        pltpu.VMEM((nz, k, wb), F32),
        pltpu.VMEM((nz, k, wb), F32),
        pltpu.VMEM((nz, 3 * k, wb), BF16),
        pltpu.VMEM((nz, 3 * k, wb), BF16),
        pltpu.VMEM((UPDATES, NW, rows // 2 + 8, 2 * k), F32),
        pltpu.VMEM((REFITS, NW, brows // 2 + 8, 2 * k), F32),
        pltpu.VMEM((nz, rows // 2, 2 * k), F32),
        pltpu.VMEM((3 * nz * rows, wb), BF16),
        pltpu.VMEM((np_, slab // 2, 2 * k), F32),
        pltpu.VMEM((np_, slab // 2, 2 * k), F32),
        pltpu.VMEM((np_, slab // 2, 2 * k), F32),
    ]
    for _ in range(4):
        scratch += [sem((NW - 1,)), sem((NW,))]
    for _ in range(2):
        scratch += [sem((2, last, 2)), sem((2, last, 2))]
    scratch += [sem((UPDATES + REFITS, NW - 1)), sem((UPDATES + REFITS, NW))]
    for _ in range(2):
        scratch += [sem((nz - 1,)), sem((nz,))]
    for _ in range(2):
        scratch += [sem((np_ - 1,)), sem((np_,))]
    vmem = pl.BlockSpec(memory_space=pltpu.VMEM)
    median, refit = pl.pallas_call(
        functools.partial(kernel, np_=np_, nz=nz),
        out_shape=(jax.ShapeDtypeStruct((slab, k), F32), jax.ShapeDtypeStruct((bdocs, k), F32)),
        in_specs=[vmem] * 7,
        out_specs=(vmem, vmem),
        scratch_shapes=scratch,
        compiler_params=pltpu.CompilerParams(
            collective_id=0, has_side_effects=True, vmem_limit_bytes=48 * 1024 * 1024
        ),
    )(counts[0], tile_mask[0], member_topics[0], start_dict[0], align_perm, base_counts, base_topics)
    return median[None, None], refit


def solution(mesh):
    np_ = mesh.shape["pert"]
    nz = mesh.shape["doc"] // NW
    return jax.shard_map(
        functools.partial(per_device, np_=np_, nz=nz),
        mesh=mesh,
        in_specs=(
            P("pert", "doc", None),
            P("pert", "doc", None),
            P("pert", "doc", None),
            P("pert", "doc", None),
            P("pert", None),
            P(("pert", "doc"), None),
            P(("pert", "doc"), None),
        ),
        out_specs=(P("doc", "pert", None, None), P(("pert", "doc"), None)),
        check_vma=False,
    )
```

```python
import functools

import jax
import jax.numpy as jnp
from jax import lax
from jax.experimental import pallas as pl
from jax.experimental.pallas import tpu as pltpu
from jax.sharding import PartitionSpec as P

UPDATES = 3
REFITS = 2
NX = 2
NC = 2
NW = NX * NC
MESH = pl.DeviceIdType.MESH
F32 = jnp.float32
BF16 = jnp.bfloat16


def sort_pairs(count):
    pairs = []
    span = 1
    while span < count:
        step = span
        while step >= 1:
            for start in range(step % span, count - step, 2 * step):
                for at in range(min(step, count - start - step)):
                    low, high = start + at, start + at + step
                    if low // (2 * span) == high // (2 * span):
                        pairs.append((low, high))
            step //= 2
        span *= 2
    return pairs


def middle(rows):
    rows = list(rows)
    for low, high in sort_pairs(len(rows)):
        rows[low], rows[high] = jnp.minimum(rows[low], rows[high]), jnp.maximum(rows[low], rows[high])
    at = len(rows) // 2
    return 0.5 * (rows[at - 1] + rows[at])


def split2(x):
    high = x.astype(BF16)
    return high, (x - high.astype(F32)).astype(BF16)


def split3(x):
    high = x.astype(BF16)
    rest = x - high.astype(F32)
    mid = rest.astype(BF16)
    return high, mid, (rest - mid.astype(F32)).astype(BF16)


def pack(x):
    half = x.shape[0] // 2
    return jnp.concatenate([x[:half], x[half:]], axis=1)


def unpack(x):
    half = x.shape[1] // 2
    return jnp.concatenate([x[:, :half], x[:, half:]], axis=0)


def turn_tall(x):
    wide = jnp.concatenate([x, jnp.zeros_like(x)], axis=1)
    return wide.T[: x.shape[1]]


def turn_flat(x):
    tall = jnp.concatenate([x, jnp.zeros_like(x)], axis=0)
    return tall.T[:, : x.shape[0]]


def dot(a, b):
    return jnp.dot(a, b, preferred_element_type=F32)


def dot_nt(a, b):
    return lax.dot_general(a, b, (((1,), (1,)), ((), ())), preferred_element_type=F32)


def kernel(
    counts_ref, mask_ref, mtop_ref, dict_ref, perm_ref, base_ref, btop_ref,
    med_ref, refit_ref,
    counts_in, mask_in, perm_in, base_in,
    masked, data4, data32, bsend, base8, bdata, mtop4, btop8, dgather, mgather, dsplit, msplit,
    mpartial, bpartial, topics_z, q3, p2_send, p2_recv, p3_recv, in_sem,
    w_send, w_recv, t_send, t_recv, x_send, x_recv, a_send, a_recv, r_send, r_recv,
    z_send, z_recv, g_send, g_recv, b_send, b_recv, u_send, u_recv, e_send, e_recv, s_send, s_recv, m_send, m_recv,
    *, np_, nz,
):
    k, wb = dict_ref.shape
    docs, bdocs = mtop_ref.shape[0], btop_ref.shape[0]
    p = lax.axis_index("pert")
    b = lax.axis_index("doc")
    xh, z, c = b // (nz * NC), (b // NC) % nz, b % NC
    w = xh * NC + c
    chunk = k // 2
    slab = wb // np_

    def w_device(at):
        return (p, (at // NC) * (nz * NC) + z * NC + at % NC)

    def z_device(at):
        return (p, xh * (nz * NC) + at * NC + c)

    def p_device(at):
        return (at, b)

    w_peers = [lax.rem(w + i, NW) for i in range(1, NW)]
    z_peers = [lax.rem(z + i, nz) for i in range(1, nz)]
    p_peers = [lax.rem(p + i, np_) for i in range(1, np_)]

    loads = [
        pltpu.make_async_copy(src, dst, in_sem.at[i])
        for i, (src, dst) in enumerate(
            (
                (mask_ref, mask_in),
                (counts_ref, counts_in),
                (dict_ref, dgather.at[z]),
                (base_ref, base_in),
                (mtop_ref, mtop4.at[w]),
                (btop_ref, btop8.at[z]),
                (perm_ref, perm_in),
            )
        )
    ]
    for load in loads:
        load.start()

    barrier = pltpu.get_barrier_semaphore()
    for peer in w_peers:
        pl.semaphore_signal(barrier, inc=1, device_id=w_device(peer), device_id_type=MESH)
    for peer in z_peers:
        pl.semaphore_signal(barrier, inc=1, device_id=z_device(peer), device_id_type=MESH)
    for peer in p_peers:
        pl.semaphore_signal(barrier, inc=1, device_id=p_device(peer), device_id_type=MESH)

    for load in loads:
        load.wait()
    tiles = mask_ref.shape[1]
    tile_width = counts_ref.shape[1] // tiles
    per_block = wb // tile_width
    tile_ids = lax.broadcasted_iota(jnp.int32, (docs, tiles), 1)
    doc_ids = b * docs + lax.broadcasted_iota(jnp.int32, (docs, tiles), 0)
    occupied = jnp.maximum(mask_in[...], (tile_ids == doc_ids % tiles).astype(jnp.int32)).astype(F32)

    for owner in range(NW):

        def mask_block(zb, carry, owner=owner):
            block = ((owner // NC) * nz + zb) * NC + owner % NC
            for j in range(per_block):
                tile = block * per_block + j
                seen = jnp.sum(jnp.where(tile_ids == tile, occupied, 0.0), axis=1, keepdims=True)
                at = pl.multiple_of(tile * tile_width, tile_width)
                masked[owner, zb, :, j * tile_width : (j + 1) * tile_width] = (
                    counts_in[:, pl.ds(at, tile_width)].astype(F32) * seen
                )
            at = pl.multiple_of(block * wb, wb)
            bsend[owner, zb] = base_in[:, pl.ds(at, wb)].astype(F32)
            return carry

        lax.fori_loop(0, nz, mask_block, 0)

    pl.semaphore_wait(barrier, NW - 1 + nz - 1 + np_ - 1)

    sends = []

    def remote(src, dst, ssem, rsem, device):
        return pltpu.make_async_remote_copy(
            src_ref=src, dst_ref=dst, send_sem=ssem, recv_sem=rsem, device_id=device, device_id_type=MESH
        )

    def start(copy):
        copy.start()
        sends.append(copy)

    last = nz // 2

    def ring_block(way, far):
        return lax.rem(z + nz - far, nz) if way == 0 else lax.rem(z + far, nz)

    def ring_copy(way, far, ch, hops):
        at = dgather.at[ring_block(way, far), pl.ds(ch * chunk, chunk), :]
        number = far + hops - 1
        return remote(
            at, at, r_send.at[way, number, ch], r_recv.at[way, number, ch], z_device(ring_block(1 - way, hops))
        )

    def ring_first():
        for ch in (0, 1):
            for way in (0, 1):
                start(ring_copy(way, 0, ch, 1))

    def ring_step(far):
        for ch in (0, 1):
            for way in (0, 1):
                if far == last and ch != way:
                    continue
                here = dgather.at[ring_block(way, far), pl.ds(ch * chunk, chunk), :]
                remote(
                    here, here, r_send.at[way, far - 1, ch], r_recv.at[way, far - 1, ch], z_device(ring_block(1 - way, 1))
                ).wait_recv()
                if far == last - 2 and ch == way:
                    start(ring_copy(way, far, ch, 2))
                if far < last - 1:
                    start(ring_copy(way, far, ch, 1))

    def blocks_at(far):
        if far == 0 or far == last:
            return [ring_block(0, far)]
        return [ring_block(0, far), ring_block(1, far)]

    def split_block(buf, out, at):
        high, low = split2(buf[at])
        out[at, 0:k] = high
        out[at, k : 2 * k] = low
        out[at, 2 * k : 3 * k] = high

    def stack_topics(topics):
        high, low = split2(topics)
        return jnp.concatenate([high, high, low], axis=1)

    def rows_of(at):
        return jnp.concatenate([data4[owner, at] for owner in range(NW)], axis=0)

    def block_term(stacked, data, split, at):
        rows = data.shape[0]
        high, low = split2(data / dot(stacked, split[at]))
        both = dot_nt(jnp.concatenate([high, low], axis=0), split[at, 0 : 2 * k])
        return both[:rows] + both[rows:]

    def column_term(split, at):
        return dot_nt(jnp.ones((16, wb), BF16), split[at, 0 : 2 * k])[:8]

    def fold(x):
        return x[:, :k] + x[:, k:]

    def exchange(partial, at, me, peers, device, sems, acc, columns, meanwhile=None):
        rows = acc.shape[0] // 2
        partial[at, me, 0:rows] = pack(fold(acc))
        sent = rows
        if columns is not None:
            partial[at, me, rows : rows + 8] = columns
            sent = rows + 8
        ssem, rsem = sems
        for i, peer in enumerate(peers):
            mine = partial.at[at, me, 0:sent]
            start(remote(mine, mine, ssem.at[at, i], rsem.at[at, me], device(peer)))
        if meanwhile is not None:
            meanwhile()
        for i, peer in enumerate(peers):
            theirs = partial.at[at, peer, 0:sent]
            remote(theirs, theirs, ssem.at[at, i], rsem.at[at, peer], device(peer)).wait_recv()
        total = partial[at, 0, 0:sent]
        for owner in range(1, len(peers) + 1):
            total = total + partial[at, owner, 0:sent]
        product = unpack(total[:rows])
        return product, (fold(total[rows : rows + 1]) if columns is not None else None)

    ring_first()
    for i, peer in enumerate(w_peers):
        start(remote(masked.at[peer], data4.at[w], w_send.at[i], w_recv.at[w], w_device(peer)))
        start(remote(mtop4.at[w], mtop4.at[w], t_send.at[i], t_recv.at[w], w_device(peer)))
    data4[w] = masked[w]
    split_block(dgather, dsplit, z)
    columns = column_term(dsplit, z)

    for far in range(1, last - 1):
        ring_step(far)
        for at in blocks_at(far):
            split_block(dgather, dsplit, at)
            columns = columns + column_term(dsplit, at)
    for i, peer in enumerate(w_peers):
        remote(mtop4.at[w], mtop4.at[peer], t_send.at[i], t_recv.at[peer], w_device(peer)).wait_recv()
        remote(masked.at[peer], data4.at[peer], w_send.at[i], w_recv.at[peer], w_device(peer)).wait_recv()
    topics = jnp.concatenate([mtop4[owner] for owner in range(NW)], axis=0)
    stacked = stack_topics(topics)
    acc = jnp.zeros((topics.shape[0], 2 * k), F32)
    for far in range(last - 1):
        for at in blocks_at(far):
            acc = acc + block_term(stacked, rows_of(at), dsplit, at)
    for far in range(last - 1, last + 1):
        ring_step(far)
        for at in blocks_at(far):
            split_block(dgather, dsplit, at)
            columns = columns + column_term(dsplit, at)
            acc = acc + block_term(stacked, rows_of(at), dsplit, at)

    def own_words():
        for i, peer in enumerate(z_peers):
            start(remote(data4.at[:, peer], data32.at[z], z_send.at[i], z_recv.at[z], z_device(peer)))
        data32[z] = data4[:, z]

    product, col_total = exchange(mpartial, 0, w, w_peers, w_device, (a_send, a_recv), acc, columns, own_words)
    topics = topics * product / col_total
    for update in range(1, UPDATES):
        stacked = stack_topics(topics)
        acc = sum(block_term(stacked, rows_of(at), dsplit, at) for at in range(nz))
        product, _ = exchange(mpartial, update, w, w_peers, w_device, (a_send, a_recv), acc, None)
        topics = topics * product / col_total

    topics_z[z] = pack(topics)
    for i, peer in enumerate(z_peers):
        start(remote(topics_z.at[z], topics_z.at[z], g_send.at[i], g_recv.at[z], z_device(peer)))
    for i, peer in enumerate(z_peers):
        remote(topics_z.at[z], topics_z.at[peer], g_send.at[i], g_recv.at[peer], z_device(peer)).wait_recv()
    for i, peer in enumerate(z_peers):
        remote(data4.at[:, peer], data32.at[peer], z_send.at[i], z_recv.at[peer], z_device(peer)).wait_recv()
    for i, peer in enumerate(z_peers):
        start(remote(bsend.at[:, peer], base8.at[z], b_send.at[i], b_recv.at[z], z_device(peer)))
        start(remote(btop8.at[z], btop8.at[z], u_send.at[i], u_recv.at[z], z_device(peer)))
    base8[z] = bsend[:, z]
    rows = NW * docs
    every = jnp.concatenate([unpack(topics_z[at]) for at in range(nz)], axis=0)

    for at in range(nz):
        recon = dot(stack_topics(every[at * rows : (at + 1) * rows]), dsplit[z])
        data = jnp.concatenate([data32[at, owner] for owner in range(NW)], axis=0)
        high, low = split2(data / recon)
        for part, piece in enumerate((high, low, high)):
            q3[(part * nz + at) * rows : (part * nz + at + 1) * rows] = piece
    wide = turn_tall(every)
    high, low = split2(wide)
    numerator = dot(jnp.concatenate([high, high, low], axis=1), q3[...])
    new_dict = dgather[z] * numerator / jnp.sum(wide, axis=1, keepdims=True)

    onehot = (lax.broadcasted_iota(jnp.int32, (k, k), 0) == perm_in[...]).astype(F32).astype(BF16)
    aligned = dot(
        jnp.concatenate(split3(turn_flat(new_dict)), axis=1), jnp.concatenate([onehot, onehot, onehot], axis=0)
    )
    for at in range(np_):
        p2_send[at] = pack(aligned[at * slab : (at + 1) * slab])
    for i, peer in enumerate(p_peers):
        start(remote(p2_send.at[peer], p2_recv.at[p], s_send.at[i], s_recv.at[p], p_device(peer)))
    p2_recv[p] = p2_send[p]
    for i, peer in enumerate(z_peers):
        remote(bsend.at[:, peer], base8.at[peer], b_send.at[i], b_recv.at[peer], z_device(peer)).wait_recv()
        remote(btop8.at[z], btop8.at[peer], u_send.at[i], u_recv.at[peer], z_device(peer)).wait_recv()
    for owner in range(NW):
        bdata[owner] = jnp.concatenate([base8[at, owner] for at in range(nz)], axis=0)
    topics = jnp.concatenate([btop8[at] for at in range(nz)], axis=0)
    stacked = stack_topics(topics)
    for i, peer in enumerate(p_peers):
        remote(p2_send.at[peer], p2_recv.at[peer], s_send.at[i], s_recv.at[peer], p_device(peer)).wait_recv()
    median = middle([p2_recv[at] for at in range(np_)])
    p3_recv[p] = median
    for i, peer in enumerate(p_peers):
        start(remote(p3_recv.at[p], p3_recv.at[p], m_send.at[i], m_recv.at[p], p_device(peer)))
    med_ref[...] = unpack(median)
    for i, peer in enumerate(p_peers):
        remote(p3_recv.at[p], p3_recv.at[peer], m_send.at[i], m_recv.at[peer], p_device(peer)).wait_recv()

    mgather[w] = turn_tall(jnp.concatenate([unpack(p3_recv[at]) for at in range(np_)], axis=0))
    for i, peer in enumerate(w_peers):
        start(remote(mgather.at[w], mgather.at[w], x_send.at[i], x_recv.at[w], w_device(peer)))
    split_block(mgather, msplit, w)
    columns = column_term(msplit, w)
    acc = block_term(stacked, bdata[w], msplit, w)
    for i, peer in enumerate(w_peers):
        remote(mgather.at[w], mgather.at[peer], x_send.at[i], x_recv.at[peer], w_device(peer)).wait_recv()
        split_block(mgather, msplit, peer)
        columns = columns + column_term(msplit, peer)
        acc = acc + block_term(stacked, bdata[peer], msplit, peer)
    product, col_total = exchange(bpartial, 0, z, z_peers, z_device, (e_send, e_recv), acc, columns)
    topics = topics * product / col_total
    for update in range(1, REFITS):
        stacked = stack_topics(topics)
        acc = sum(block_term(stacked, bdata[at], msplit, at) for at in range(NW))
        product, _ = exchange(bpartial, update, z, z_peers, z_device, (e_send, e_recv), acc, None)
        topics = topics * product / col_total
    own = topics[0:bdocs]
    for at in range(1, nz):
        own = jnp.where(z == at, topics[at * bdocs : (at + 1) * bdocs], own)
    refit_ref[...] = own

    for copy in sends:
        copy.wait_send()


def per_device(counts, tile_mask, member_topics, start_dict, align_perm, base_counts, base_topics, *, np_, nz):
    docs, bdocs = counts.shape[1], base_counts.shape[0]
    wb, k = start_dict.shape[1:]
    slab = wb // np_
    last = nz // 2
    rows, brows = NW * docs, nz * bdocs
    sem = pltpu.SemaphoreType.DMA
    scratch = [
        pltpu.VMEM(counts.shape[1:], counts.dtype),
        pltpu.VMEM(tile_mask.shape[1:], tile_mask.dtype),
        pltpu.VMEM(align_perm.shape, align_perm.dtype),
        pltpu.VMEM(base_counts.shape, base_counts.dtype),
        pltpu.VMEM((NW, nz, docs, wb), F32),
        pltpu.VMEM((NW, nz, docs, wb), F32),
        pltpu.VMEM((nz, NW, docs, wb), F32),
        pltpu.VMEM((NW, nz, bdocs, wb), F32),
        pltpu.VMEM((nz, NW, bdocs, wb), F32),
        pltpu.VMEM((NW, brows, wb), F32),
        pltpu.VMEM((NW, docs, k), F32),
        pltpu.VMEM((nz, bdocs, k), F32),
        pltpu.VMEM((nz, k, wb), F32),
        pltpu.VMEM((NW, k, wb), F32),
        pltpu.VMEM((nz, 3 * k, wb), BF16),
        pltpu.VMEM((NW, 3 * k, wb), BF16),
        pltpu.VMEM((UPDATES, NW, rows // 2 + 8, 2 * k), F32),
        pltpu.VMEM((REFITS, nz, brows // 2 + 8, 2 * k), F32),
        pltpu.VMEM((nz, rows // 2, 2 * k), F32),
        pltpu.VMEM((3 * nz * rows, wb), BF16),
        pltpu.VMEM((np_, slab // 2, 2 * k), F32),
        pltpu.VMEM((np_, slab // 2, 2 * k), F32),
        pltpu.VMEM((np_, slab // 2, 2 * k), F32),
        sem((7,)),
    ]
    for _ in range(3):
        scratch += [sem((NW - 1,)), sem((NW,))]
    scratch += [sem((UPDATES, NW - 1)), sem((UPDATES, NW))]
    scratch += [sem((2, last, 2)), sem((2, last, 2))]
    for _ in range(4):
        scratch += [sem((nz - 1,)), sem((nz,))]
    scratch += [sem((REFITS, nz - 1)), sem((REFITS, nz))]
    for _ in range(2):
        scratch += [sem((np_ - 1,)), sem((np_,))]
    here = pl.BlockSpec(memory_space=pl.ANY)
    vmem = pl.BlockSpec(memory_space=pltpu.VMEM)
    median, refit = pl.pallas_call(
        functools.partial(kernel, np_=np_, nz=nz),
        out_shape=(jax.ShapeDtypeStruct((slab, k), F32), jax.ShapeDtypeStruct((bdocs, k), F32)),
        in_specs=[here] * 7,
        out_specs=(vmem, vmem),
        scratch_shapes=scratch,
        compiler_params=pltpu.CompilerParams(collective_id=0, has_side_effects=True),
    )(counts[0], tile_mask[0], member_topics[0], start_dict[0].T, align_perm, base_counts, base_topics)
    return median[None, None], refit


def solution(mesh):
    np_ = mesh.shape["pert"]
    nz = mesh.shape["doc"] // NW
    return jax.shard_map(
        functools.partial(per_device, np_=np_, nz=nz),
        mesh=mesh,
        in_specs=(
            P("pert", "doc", None),
            P("pert", "doc", None),
            P("pert", "doc", None),
            P("pert", "doc", None),
            P("pert", None),
            P(("pert", "doc"), None),
            P(("pert", "doc"), None),
        ),
        out_specs=(P("doc", "pert", None, None), P(("pert", "doc"), None)),
        check_vma=False,
    )
```

```python
import functools

import jax
import jax.numpy as jnp
from jax import lax
from jax.experimental import pallas as pl
from jax.experimental.pallas import tpu as pltpu
from jax.sharding import PartitionSpec as P

UPDATES = 3
REFITS = 2
NX = 2
NC = 2
NW = NX * NC
MESH = pl.DeviceIdType.MESH
F32 = jnp.float32
BF16 = jnp.bfloat16


def sort_pairs(count):
    pairs = []
    span = 1
    while span < count:
        step = span
        while step >= 1:
            for start in range(step % span, count - step, 2 * step):
                for at in range(min(step, count - start - step)):
                    low, high = start + at, start + at + step
                    if low // (2 * span) == high // (2 * span):
                        pairs.append((low, high))
            step //= 2
        span *= 2
    return pairs


def middle(rows):
    rows = list(rows)
    for low, high in sort_pairs(len(rows)):
        rows[low], rows[high] = jnp.minimum(rows[low], rows[high]), jnp.maximum(rows[low], rows[high])
    at = len(rows) // 2
    return 0.5 * (rows[at - 1] + rows[at])


def split2(x):
    high = x.astype(BF16)
    return high, (x - high.astype(F32)).astype(BF16)


def split3(x):
    high = x.astype(BF16)
    rest = x - high.astype(F32)
    mid = rest.astype(BF16)
    return high, mid, (rest - mid.astype(F32)).astype(BF16)


def pack(x):
    half = x.shape[0] // 2
    return jnp.concatenate([x[:half], x[half:]], axis=1)


def unpack(x):
    half = x.shape[1] // 2
    return jnp.concatenate([x[:, :half], x[:, half:]], axis=0)


def turn_tall(x):
    wide = jnp.concatenate([x, jnp.zeros_like(x)], axis=1)
    return wide.T[: x.shape[1]]


def turn_flat(x):
    tall = jnp.concatenate([x, jnp.zeros_like(x)], axis=0)
    return tall.T[:, : x.shape[0]]


def dot(a, b):
    return jnp.dot(a, b, preferred_element_type=F32)


def dot_nt(a, b):
    return lax.dot_general(a, b, (((1,), (1,)), ((), ())), preferred_element_type=F32)


def kernel(
    counts_ref, mask_ref, mtop_ref, dict_ref, perm_ref, base_ref, btop_ref,
    med_ref, refit_ref,
    counts_in, mask_in, perm_in, base_in,
    masked, data4, data32, bsend, base8, bdata, mtop4, btop8, dgather, mgather, dsplit, msplit,
    mpartial, bpartial, topics_z, q3, p2_send, p2_recv, p3_recv, in_sem,
    w_send, w_recv, t_send, t_recv, x_send, x_recv, a_send, a_recv, r_send, r_recv,
    z_send, z_recv, g_send, g_recv, b_send, b_recv, u_send, u_recv, e_send, e_recv, s_send, s_recv, m_send, m_recv,
    *, np_, nz,
):
    k, wb = dict_ref.shape
    docs, bdocs = mtop_ref.shape[0], btop_ref.shape[0]
    p = lax.axis_index("pert")
    b = lax.axis_index("doc")
    xh, z, c = b // (nz * NC), (b // NC) % nz, b % NC
    w = xh * NC + c
    chunk = k // 4
    slab = wb // np_

    def w_device(at):
        return (p, (at // NC) * (nz * NC) + z * NC + at % NC)

    def z_device(at):
        return (p, xh * (nz * NC) + at * NC + c)

    def p_device(at):
        return (at, b)

    w_peers = [lax.rem(w + i, NW) for i in range(1, NW)]
    z_peers = [lax.rem(z + i, nz) for i in range(1, nz)]
    p_peers = [lax.rem(p + i, np_) for i in range(1, np_)]

    loads = [
        pltpu.make_async_copy(src, dst, in_sem.at[i])
        for i, (src, dst) in enumerate(
            (
                (dict_ref, dgather.at[z]),
                (mask_ref, mask_in),
                (counts_ref, counts_in),
                (base_ref, base_in),
                (mtop_ref, mtop4.at[w]),
                (btop_ref, btop8.at[z]),
                (perm_ref, perm_in),
            )
        )
    ]
    for load in loads:
        load.start()

    barrier = pltpu.get_barrier_semaphore()
    for peer in w_peers:
        pl.semaphore_signal(barrier, inc=1, device_id=w_device(peer), device_id_type=MESH)
    for peer in z_peers:
        pl.semaphore_signal(barrier, inc=1, device_id=z_device(peer), device_id_type=MESH)
    for peer in p_peers:
        pl.semaphore_signal(barrier, inc=1, device_id=p_device(peer), device_id_type=MESH)

    loads[0].wait()
    pl.semaphore_wait(barrier, NW - 1 + nz - 1 + np_ - 1)

    sends = []

    def remote(src, dst, ssem, rsem, device):
        return pltpu.make_async_remote_copy(
            src_ref=src, dst_ref=dst, send_sem=ssem, recv_sem=rsem, device_id=device, device_id_type=MESH
        )

    def start(copy):
        copy.start()
        sends.append(copy)

    last = nz // 2

    def ring_block(way, far):
        return lax.rem(z + nz - far, nz) if way == 0 else lax.rem(z + far, nz)

    def ring_copy(way, far, ch, hops):
        at = dgather.at[ring_block(way, far), pl.ds(ch * chunk, chunk), :]
        number = far + hops - 1
        return remote(
            at, at, r_send.at[way, number, ch], r_recv.at[way, number, ch], z_device(ring_block(1 - way, hops))
        )

    def ring_first():
        for ch in range(4):
            for way in (0, 1):
                start(ring_copy(way, 0, ch, 1))

    def ring_step(far):
        for ch in range(4):
            for way in (0, 1):
                if far == last and ch // 2 != way:
                    continue
                here = dgather.at[ring_block(way, far), pl.ds(ch * chunk, chunk), :]
                remote(
                    here, here, r_send.at[way, far - 1, ch], r_recv.at[way, far - 1, ch], z_device(ring_block(1 - way, 1))
                ).wait_recv()
                if far == last - 2 and ch // 2 == way:
                    start(ring_copy(way, far, ch, 2))
                if far < last - 1:
                    start(ring_copy(way, far, ch, 1))

    def blocks_at(far):
        if far == 0 or far == last:
            return [ring_block(0, far)]
        return [ring_block(0, far), ring_block(1, far)]

    def split_block(buf, out, at):
        high, low = split2(buf[at])
        out[at, 0:k] = high
        out[at, k : 2 * k] = low
        out[at, 2 * k : 3 * k] = high

    def stack_topics(topics):
        high, low = split2(topics)
        return jnp.concatenate([high, high, low], axis=1)

    def rows_of(at):
        return jnp.concatenate([data4[owner, at] for owner in range(NW)], axis=0)

    def block_term(stacked, data, split, at):
        rows = data.shape[0]
        high, low = split2(data / dot(stacked, split[at]))
        both = dot_nt(jnp.concatenate([high, low], axis=0), split[at, 0 : 2 * k])
        return both[:rows] + both[rows:]

    def column_term(split, at):
        return dot_nt(jnp.ones((16, wb), BF16), split[at, 0 : 2 * k])[:8]

    def fold(x):
        return x[:, :k] + x[:, k:]

    def exchange(partial, at, me, peers, device, sems, acc, columns, meanwhile=None):
        rows = acc.shape[0] // 2
        partial[at, me, 0:rows] = pack(fold(acc))
        sent = rows
        if columns is not None:
            partial[at, me, rows : rows + 8] = columns
            sent = rows + 8
        ssem, rsem = sems
        for i, peer in enumerate(peers):
            mine = partial.at[at, me, 0:sent]
            start(remote(mine, mine, ssem.at[at, i], rsem.at[at, me], device(peer)))
        if meanwhile is not None:
            meanwhile()
        for i, peer in enumerate(peers):
            theirs = partial.at[at, peer, 0:sent]
            remote(theirs, theirs, ssem.at[at, i], rsem.at[at, peer], device(peer)).wait_recv()
        total = partial[at, 0, 0:sent]
        for owner in range(1, len(peers) + 1):
            total = total + partial[at, owner, 0:sent]
        product = unpack(total[:rows])
        return product, (fold(total[rows : rows + 1]) if columns is not None else None)

    ring_first()
    for load in loads[1:]:
        load.wait()
    tiles = mask_ref.shape[1]
    tile_width = counts_ref.shape[1] // tiles
    per_block = wb // tile_width
    tile_ids = lax.broadcasted_iota(jnp.int32, (docs, tiles), 1)
    doc_ids = b * docs + lax.broadcasted_iota(jnp.int32, (docs, tiles), 0)
    occupied = jnp.maximum(mask_in[...], (tile_ids == doc_ids % tiles).astype(jnp.int32)).astype(F32)

    for owner in range(NW):

        def mask_block(zb, carry, owner=owner):
            block = ((owner // NC) * nz + zb) * NC + owner % NC
            for j in range(per_block):
                tile = block * per_block + j
                seen = jnp.sum(jnp.where(tile_ids == tile, occupied, 0.0), axis=1, keepdims=True)
                at = pl.multiple_of(tile * tile_width, tile_width)
                masked[owner, zb, :, j * tile_width : (j + 1) * tile_width] = (
                    counts_in[:, pl.ds(at, tile_width)].astype(F32) * seen
                )
            at = pl.multiple_of(block * wb, wb)
            bsend[owner, zb] = base_in[:, pl.ds(at, wb)].astype(F32)
            return carry

        lax.fori_loop(0, nz, mask_block, 0)
    for i, peer in enumerate(w_peers):
        start(remote(masked.at[peer], data4.at[w], w_send.at[i], w_recv.at[w], w_device(peer)))
        start(remote(mtop4.at[w], mtop4.at[w], t_send.at[i], t_recv.at[w], w_device(peer)))
    for far in range(1, last - 1):
        ring_step(far)
    data4[w] = masked[w]
    columns = jnp.zeros((8, 2 * k), F32)
    for far in range(last - 1):
        for at in blocks_at(far):
            split_block(dgather, dsplit, at)
            columns = columns + column_term(dsplit, at)

    for i, peer in enumerate(w_peers):
        remote(mtop4.at[w], mtop4.at[peer], t_send.at[i], t_recv.at[peer], w_device(peer)).wait_recv()
        remote(masked.at[peer], data4.at[peer], w_send.at[i], w_recv.at[peer], w_device(peer)).wait_recv()
    topics = jnp.concatenate([mtop4[owner] for owner in range(NW)], axis=0)
    stacked = stack_topics(topics)
    acc = jnp.zeros((topics.shape[0], 2 * k), F32)
    for far in range(last - 1):
        for at in blocks_at(far):
            acc = acc + block_term(stacked, rows_of(at), dsplit, at)
    for far in range(last - 1, last + 1):
        ring_step(far)
        for at in blocks_at(far):
            split_block(dgather, dsplit, at)
            columns = columns + column_term(dsplit, at)
            acc = acc + block_term(stacked, rows_of(at), dsplit, at)

    def own_words():
        for i, peer in enumerate(z_peers):
            start(remote(data4.at[:, peer], data32.at[z], z_send.at[i], z_recv.at[z], z_device(peer)))
        data32[z] = data4[:, z]

    product, col_total = exchange(mpartial, 0, w, w_peers, w_device, (a_send, a_recv), acc, columns, own_words)
    topics = topics * product / col_total
    for update in range(1, UPDATES):
        stacked = stack_topics(topics)
        acc = sum(block_term(stacked, rows_of(at), dsplit, at) for at in range(nz))
        product, _ = exchange(mpartial, update, w, w_peers, w_device, (a_send, a_recv), acc, None)
        topics = topics * product / col_total

    topics_z[z] = pack(topics)
    for i, peer in enumerate(z_peers):
        start(remote(topics_z.at[z], topics_z.at[z], g_send.at[i], g_recv.at[z], z_device(peer)))
    for i, peer in enumerate(z_peers):
        remote(topics_z.at[z], topics_z.at[peer], g_send.at[i], g_recv.at[peer], z_device(peer)).wait_recv()
    for i, peer in enumerate(z_peers):
        remote(data4.at[:, peer], data32.at[peer], z_send.at[i], z_recv.at[peer], z_device(peer)).wait_recv()
    for i, peer in enumerate(z_peers):
        start(remote(bsend.at[:, peer], base8.at[z], b_send.at[i], b_recv.at[z], z_device(peer)))
        start(remote(btop8.at[z], btop8.at[z], u_send.at[i], u_recv.at[z], z_device(peer)))
    base8[z] = bsend[:, z]
    rows = NW * docs
    every = jnp.concatenate([unpack(topics_z[at]) for at in range(nz)], axis=0)

    for at in range(nz):
        recon = dot(stack_topics(every[at * rows : (at + 1) * rows]), dsplit[z])
        data = jnp.concatenate([data32[at, owner] for owner in range(NW)], axis=0)
        high, low = split2(data / recon)
        for part, piece in enumerate((high, low, high)):
            q3[(part * nz + at) * rows : (part * nz + at + 1) * rows] = piece
    wide = turn_tall(every)
    high, low = split2(wide)
    numerator = dot(jnp.concatenate([high, high, low], axis=1), q3[...])
    new_dict = dgather[z] * numerator / jnp.sum(wide, axis=1, keepdims=True)

    onehot = (lax.broadcasted_iota(jnp.int32, (k, k), 0) == perm_in[...]).astype(F32).astype(BF16)
    aligned = dot(
        jnp.concatenate(split3(turn_flat(new_dict)), axis=1), jnp.concatenate([onehot, onehot, onehot], axis=0)
    )
    for at in range(np_):
        p2_send[at] = pack(aligned[at * slab : (at + 1) * slab])
    for i, peer in enumerate(p_peers):
        start(remote(p2_send.at[peer], p2_recv.at[p], s_send.at[i], s_recv.at[p], p_device(peer)))
    p2_recv[p] = p2_send[p]
    for i, peer in enumerate(p_peers):
        remote(p2_send.at[peer], p2_recv.at[peer], s_send.at[i], s_recv.at[peer], p_device(peer)).wait_recv()
    median = middle([p2_recv[at] for at in range(np_)])
    p3_recv[p] = median
    for i, peer in enumerate(p_peers):
        start(remote(p3_recv.at[p], p3_recv.at[p], m_send.at[i], m_recv.at[p], p_device(peer)))
    med_ref[...] = unpack(median)
    for i, peer in enumerate(z_peers):
        remote(bsend.at[:, peer], base8.at[peer], b_send.at[i], b_recv.at[peer], z_device(peer)).wait_recv()
        remote(btop8.at[z], btop8.at[peer], u_send.at[i], u_recv.at[peer], z_device(peer)).wait_recv()
    for owner in range(NW):
        bdata[owner] = jnp.concatenate([base8[at, owner] for at in range(nz)], axis=0)
    topics = jnp.concatenate([btop8[at] for at in range(nz)], axis=0)
    stacked = stack_topics(topics)
    for i, peer in enumerate(p_peers):
        remote(p3_recv.at[p], p3_recv.at[peer], m_send.at[i], m_recv.at[peer], p_device(peer)).wait_recv()

    mgather[w] = turn_tall(jnp.concatenate([unpack(p3_recv[at]) for at in range(np_)], axis=0))
    for i, peer in enumerate(w_peers):
        start(remote(mgather.at[w], mgather.at[w], x_send.at[i], x_recv.at[w], w_device(peer)))
    split_block(mgather, msplit, w)
    columns = column_term(msplit, w)
    acc = block_term(stacked, bdata[w], msplit, w)
    for i, peer in enumerate(w_peers):
        remote(mgather.at[w], mgather.at[peer], x_send.at[i], x_recv.at[peer], w_device(peer)).wait_recv()
        split_block(mgather, msplit, peer)
        columns = columns + column_term(msplit, peer)
        acc = acc + block_term(stacked, bdata[peer], msplit, peer)
    product, col_total = exchange(bpartial, 0, z, z_peers, z_device, (e_send, e_recv), acc, columns)
    topics = topics * product / col_total
    for update in range(1, REFITS):
        stacked = stack_topics(topics)
        acc = sum(block_term(stacked, bdata[at], msplit, at) for at in range(NW))
        product, _ = exchange(bpartial, update, z, z_peers, z_device, (e_send, e_recv), acc, None)
        topics = topics * product / col_total
    own = topics[0:bdocs]
    for at in range(1, nz):
        own = jnp.where(z == at, topics[at * bdocs : (at + 1) * bdocs], own)
    refit_ref[...] = own

    for copy in sends:
        copy.wait_send()


def per_device(counts, tile_mask, member_topics, start_dict, align_perm, base_counts, base_topics, *, np_, nz):
    docs, bdocs = counts.shape[1], base_counts.shape[0]
    wb, k = start_dict.shape[1:]
    slab = wb // np_
    last = nz // 2
    rows, brows = NW * docs, nz * bdocs
    sem = pltpu.SemaphoreType.DMA
    scratch = [
        pltpu.VMEM(counts.shape[1:], counts.dtype),
        pltpu.VMEM(tile_mask.shape[1:], tile_mask.dtype),
        pltpu.VMEM(align_perm.shape, align_perm.dtype),
        pltpu.VMEM(base_counts.shape, base_counts.dtype),
        pltpu.VMEM((NW, nz, docs, wb), F32),
        pltpu.VMEM((NW, nz, docs, wb), F32),
        pltpu.VMEM((nz, NW, docs, wb), F32),
        pltpu.VMEM((NW, nz, bdocs, wb), F32),
        pltpu.VMEM((nz, NW, bdocs, wb), F32),
        pltpu.VMEM((NW, brows, wb), F32),
        pltpu.VMEM((NW, docs, k), F32),
        pltpu.VMEM((nz, bdocs, k), F32),
        pltpu.VMEM((nz, k, wb), F32),
        pltpu.VMEM((NW, k, wb), F32),
        pltpu.VMEM((nz, 3 * k, wb), BF16),
        pltpu.VMEM((NW, 3 * k, wb), BF16),
        pltpu.VMEM((UPDATES, NW, rows // 2 + 8, 2 * k), F32),
        pltpu.VMEM((REFITS, nz, brows // 2 + 8, 2 * k), F32),
        pltpu.VMEM((nz, rows // 2, 2 * k), F32),
        pltpu.VMEM((3 * nz * rows, wb), BF16),
        pltpu.VMEM((np_, slab // 2, 2 * k), F32),
        pltpu.VMEM((np_, slab // 2, 2 * k), F32),
        pltpu.VMEM((np_, slab // 2, 2 * k), F32),
        sem((7,)),
    ]
    for _ in range(3):
        scratch += [sem((NW - 1,)), sem((NW,))]
    scratch += [sem((UPDATES, NW - 1)), sem((UPDATES, NW))]
    scratch += [sem((2, last, 4)), sem((2, last, 4))]
    for _ in range(4):
        scratch += [sem((nz - 1,)), sem((nz,))]
    scratch += [sem((REFITS, nz - 1)), sem((REFITS, nz))]
    for _ in range(2):
        scratch += [sem((np_ - 1,)), sem((np_,))]
    here = pl.BlockSpec(memory_space=pl.ANY)
    vmem = pl.BlockSpec(memory_space=pltpu.VMEM)
    median, refit = pl.pallas_call(
        functools.partial(kernel, np_=np_, nz=nz),
        out_shape=(jax.ShapeDtypeStruct((slab, k), F32), jax.ShapeDtypeStruct((bdocs, k), F32)),
        in_specs=[here] * 7,
        out_specs=(vmem, vmem),
        scratch_shapes=scratch,
        compiler_params=pltpu.CompilerParams(collective_id=0, has_side_effects=True),
    )(counts[0], tile_mask[0], member_topics[0], start_dict[0].T, align_perm, base_counts, base_topics)
    return median[None, None], refit


def solution(mesh):
    np_ = mesh.shape["pert"]
    nz = mesh.shape["doc"] // NW
    return jax.shard_map(
        functools.partial(per_device, np_=np_, nz=nz),
        mesh=mesh,
        in_specs=(
            P("pert", "doc", None),
            P("pert", "doc", None),
            P("pert", "doc", None),
            P("pert", "doc", None),
            P("pert", None),
            P(("pert", "doc"), None),
            P(("pert", "doc"), None),
        ),
        out_specs=(P("doc", "pert", None, None), P(("pert", "doc"), None)),
        check_vma=False,
    )
```

```python
import functools

import jax
import jax.numpy as jnp
from jax import lax
from jax.experimental import pallas as pl
from jax.experimental.pallas import tpu as pltpu
from jax.sharding import PartitionSpec as P

UPDATES = 3
REFITS = 2
NX = 2
NC = 2
NW = NX * NC
MESH = pl.DeviceIdType.MESH
F32 = jnp.float32
BF16 = jnp.bfloat16


def sort_pairs(count):
    pairs = []
    span = 1
    while span < count:
        step = span
        while step >= 1:
            for start in range(step % span, count - step, 2 * step):
                for at in range(min(step, count - start - step)):
                    low, high = start + at, start + at + step
                    if low // (2 * span) == high // (2 * span):
                        pairs.append((low, high))
            step //= 2
        span *= 2
    return pairs


def middle(rows):
    rows = list(rows)
    for low, high in sort_pairs(len(rows)):
        rows[low], rows[high] = jnp.minimum(rows[low], rows[high]), jnp.maximum(rows[low], rows[high])
    at = len(rows) // 2
    return 0.5 * (rows[at - 1] + rows[at])


def split2(x):
    high = x.astype(BF16)
    return high, (x - high.astype(F32)).astype(BF16)


def split3(x):
    high = x.astype(BF16)
    rest = x - high.astype(F32)
    mid = rest.astype(BF16)
    return high, mid, (rest - mid.astype(F32)).astype(BF16)


def pack(x):
    half = x.shape[0] // 2
    return jnp.concatenate([x[:half], x[half:]], axis=1)


def unpack(x):
    half = x.shape[1] // 2
    return jnp.concatenate([x[:, :half], x[:, half:]], axis=0)


def turn_tall(x):
    wide = jnp.concatenate([x, jnp.zeros_like(x)], axis=1)
    return wide.T[: x.shape[1]]


def turn_flat(x):
    tall = jnp.concatenate([x, jnp.zeros_like(x)], axis=0)
    return tall.T[:, : x.shape[0]]


def dot(a, b):
    return jnp.dot(a, b, preferred_element_type=F32)


def dot_nt(a, b):
    return lax.dot_general(a, b, (((1,), (1,)), ((), ())), preferred_element_type=F32)


def kernel(
    counts_ref, mask_ref, mtop_ref, dict_ref, perm_ref, base_ref, btop_ref,
    med_ref, refit_ref,
    counts_in, mask_in, perm_in, base_in,
    masked, data4, data32, bsend, base8, bdata, mtop4, btop8, dgather, mgather, dsplit, msplit,
    mpartial, bpartial, topics_z, q3, p2_send, p2_recv, p3_recv, in_sem, here_sem, line_sem,
    w_send, w_recv, t_send, t_recv, x_send, x_recv, a_send, a_recv, r_send, r_recv,
    z_send, z_recv, g_send, g_recv, b_send, b_recv, u_send, u_recv, e_send, e_recv, s_send, s_recv, m_send, m_recv,
    *, np_, nz,
):
    k, wb = dict_ref.shape
    docs, bdocs = mtop_ref.shape[0], btop_ref.shape[0]
    p = lax.axis_index("pert")
    b = lax.axis_index("doc")
    xh, z, c = b // (nz * NC), (b // NC) % nz, b % NC
    w = xh * NC + c
    chunk, chunk2 = k // 4, k // 2
    slab = wb // np_

    def w_device(at):
        return (p, (at // NC) * (nz * NC) + z * NC + at % NC)

    def z_device(at):
        return (p, xh * (nz * NC) + at * NC + c)

    def p_device(at):
        return (at, b)

    w_peers = [lax.rem(w + i, NW) for i in range(1, NW)]
    z_peers = [lax.rem(z + i, nz) for i in range(1, nz)]
    p_peers = [lax.rem(p + i, np_) for i in range(1, np_)]

    loads = [
        pltpu.make_async_copy(src, dst, in_sem.at[i])
        for i, (src, dst) in enumerate(
            (
                (dict_ref, dgather.at[z]),
                (mask_ref, mask_in),
                (counts_ref, counts_in),
                (base_ref, base_in),
                (mtop_ref, mtop4.at[w]),
                (btop_ref, btop8.at[z]),
                (perm_ref, perm_in),
            )
        )
    ]
    for load in loads:
        load.start()

    barrier = pltpu.get_barrier_semaphore()
    ny = np_ // NX
    xl, y = p // ny, p % ny
    y_next = [p_device(xl * ny + lax.rem(y + step, ny)) for step in (1, ny - 1)]
    x_across = p_device((NX - 1 - xl) * ny + y)
    near = [w_device(peer) for peer in w_peers] + [z_device(z_peers[0]), z_device(z_peers[-1])] + y_next + [x_across]
    for device in near:
        pl.semaphore_signal(barrier, inc=1, device_id=device, device_id_type=MESH)

    loads[0].wait()
    pl.semaphore_wait(barrier, len(near))

    def tell(stage):
        if stage > 0:
            for way in (0, 1):
                pl.semaphore_wait(here_sem.at[way, stage - 1], 1)
        if stage < ny // 2 - 1:
            for way in (0, 1):
                pl.semaphore_signal(here_sem.at[way, stage], inc=1, device_id=y_next[way], device_id_type=MESH)
        else:
            pl.semaphore_signal(line_sem.at[0], inc=1, device_id=x_across, device_id_type=MESH)

    tell(0)

    sends = []

    def remote(src, dst, ssem, rsem, device):
        return pltpu.make_async_remote_copy(
            src_ref=src, dst_ref=dst, send_sem=ssem, recv_sem=rsem, device_id=device, device_id_type=MESH
        )

    def start(copy):
        copy.start()
        sends.append(copy)

    last = nz // 2

    def ring_block(way, far):
        return lax.rem(z + nz - far, nz) if way == 0 else lax.rem(z + far, nz)

    def ring_copy(way, far, ch, hops):
        at = dgather.at[ring_block(way, far), pl.ds(ch * chunk, chunk), :]
        number = far + hops - 1
        return remote(
            at, at, r_send.at[way, number, ch], r_recv.at[way, number, ch], z_device(ring_block(1 - way, hops))
        )

    def ring_first():
        for ch in range(4):
            for way in (0, 1):
                start(ring_copy(way, 0, ch, 1))

    def ring_step(far):
        for ch in range(4):
            for way in (0, 1):
                if far == last and ch // 2 != way:
                    continue
                here = dgather.at[ring_block(way, far), pl.ds(ch * chunk, chunk), :]
                remote(
                    here, here, r_send.at[way, far - 1, ch], r_recv.at[way, far - 1, ch], z_device(ring_block(1 - way, 1))
                ).wait_recv()
                if far < last - 1:
                    start(ring_copy(way, far, ch, 1))
            if far == last - 2:
                start(ring_copy(ch // 2, far, ch, 2))

    def blocks_at(far):
        if far == 0 or far == last:
            return [ring_block(0, far)]
        return [ring_block(0, far), ring_block(1, far)]

    def split_block(buf, out, at):
        high, low = split2(buf[at])
        out[at, 0:k] = high
        out[at, k : 2 * k] = low
        out[at, 2 * k : 3 * k] = high

    def stack_topics(topics):
        high, low = split2(topics)
        return jnp.concatenate([high, high, low], axis=1)

    def rows_of(at):
        return jnp.concatenate([data4[owner, at] for owner in range(NW)], axis=0)

    def block_term(stacked, data, split, at):
        rows = data.shape[0]
        high, low = split2(data / dot(stacked, split[at]))
        both = dot_nt(jnp.concatenate([high, low], axis=0), split[at, 0 : 2 * k])
        return both[:rows] + both[rows:]

    def column_term(split, at):
        return dot_nt(jnp.ones((16, wb), BF16), split[at, 0 : 2 * k])[:8]

    def fold(x):
        return x[:, :k] + x[:, k:]

    def exchange(partial, at, me, peers, device, sems, acc, columns, meanwhile=None):
        rows = acc.shape[0] // 2
        partial[at, me, 0:rows] = pack(fold(acc))
        sent = rows
        if columns is not None:
            partial[at, me, rows : rows + 8] = columns
            sent = rows + 8
        ssem, rsem = sems
        for i, peer in enumerate(peers):
            mine = partial.at[at, me, 0:sent]
            start(remote(mine, mine, ssem.at[at, i], rsem.at[at, me], device(peer)))
        if meanwhile is not None:
            meanwhile()
        for i, peer in enumerate(peers):
            theirs = partial.at[at, peer, 0:sent]
            remote(theirs, theirs, ssem.at[at, i], rsem.at[at, peer], device(peer)).wait_recv()
        total = partial[at, 0, 0:sent]
        for owner in range(1, len(peers) + 1):
            total = total + partial[at, owner, 0:sent]
        product = unpack(total[:rows])
        return product, (fold(total[rows : rows + 1]) if columns is not None else None)

    ring_first()
    for load in loads[1:]:
        load.wait()
    tiles = mask_ref.shape[1]
    tile_width = counts_ref.shape[1] // tiles
    per_block = wb // tile_width
    tile_ids = lax.broadcasted_iota(jnp.int32, (docs, tiles), 1)
    doc_ids = b * docs + lax.broadcasted_iota(jnp.int32, (docs, tiles), 0)
    occupied = jnp.maximum(mask_in[...], (tile_ids == doc_ids % tiles).astype(jnp.int32)).astype(F32)

    for owner in range(NW):

        def mask_block(zb, carry, owner=owner):
            block = ((owner // NC) * nz + zb) * NC + owner % NC
            for j in range(per_block):
                tile = block * per_block + j
                seen = jnp.sum(jnp.where(tile_ids == tile, occupied, 0.0), axis=1, keepdims=True)
                at = pl.multiple_of(tile * tile_width, tile_width)
                masked[owner, zb, :, j * tile_width : (j + 1) * tile_width] = (
                    counts_in[:, pl.ds(at, tile_width)].astype(F32) * seen
                )
            at = pl.multiple_of(block * wb, wb)
            bsend[owner, zb] = base_in[:, pl.ds(at, wb)].astype(F32)
            return carry

        lax.fori_loop(0, nz, mask_block, 0)
    for i, peer in enumerate(w_peers):
        start(remote(masked.at[peer], data4.at[w], w_send.at[i], w_recv.at[w], w_device(peer)))
        start(remote(mtop4.at[w], mtop4.at[w], t_send.at[i], t_recv.at[w], w_device(peer)))
    for far in range(1, last - 1):
        ring_step(far)
    data4[w] = masked[w]
    columns = jnp.zeros((8, 2 * k), F32)
    for far in range(last - 1):
        for at in blocks_at(far):
            split_block(dgather, dsplit, at)
            columns = columns + column_term(dsplit, at)

    for i, peer in enumerate(w_peers):
        remote(mtop4.at[w], mtop4.at[peer], t_send.at[i], t_recv.at[peer], w_device(peer)).wait_recv()
        remote(masked.at[peer], data4.at[peer], w_send.at[i], w_recv.at[peer], w_device(peer)).wait_recv()
    topics = jnp.concatenate([mtop4[owner] for owner in range(NW)], axis=0)
    stacked = stack_topics(topics)
    acc = jnp.zeros((topics.shape[0], 2 * k), F32)
    for far in range(last - 1):
        for at in blocks_at(far):
            acc = acc + block_term(stacked, rows_of(at), dsplit, at)
    for far in range(last - 1, last + 1):
        ring_step(far)
        for at in blocks_at(far):
            split_block(dgather, dsplit, at)
            columns = columns + column_term(dsplit, at)
            acc = acc + block_term(stacked, rows_of(at), dsplit, at)

    def own_words():
        for i, peer in enumerate(z_peers):
            start(remote(data4.at[:, peer], data32.at[z], z_send.at[i], z_recv.at[z], z_device(peer)))
        data32[z] = data4[:, z]
        tell(1)

    product, col_total = exchange(mpartial, 0, w, w_peers, w_device, (a_send, a_recv), acc, columns, own_words)
    topics = topics * product / col_total
    for update in range(1, UPDATES):
        stacked = stack_topics(topics)
        acc = sum(block_term(stacked, rows_of(at), dsplit, at) for at in range(nz))
        product, _ = exchange(
            mpartial, update, w, w_peers, w_device, (a_send, a_recv), acc, None, functools.partial(tell, update + 1)
        )
        topics = topics * product / col_total

    topics_z[z] = pack(topics)
    for i, peer in enumerate(z_peers):
        start(remote(topics_z.at[z], topics_z.at[z], g_send.at[i], g_recv.at[z], z_device(peer)))
    for i, peer in enumerate(z_peers):
        remote(topics_z.at[z], topics_z.at[peer], g_send.at[i], g_recv.at[peer], z_device(peer)).wait_recv()
    for i, peer in enumerate(z_peers):
        remote(data4.at[:, peer], data32.at[peer], z_send.at[i], z_recv.at[peer], z_device(peer)).wait_recv()
    for i, peer in enumerate(z_peers):
        start(remote(bsend.at[:, peer], base8.at[z], b_send.at[i], b_recv.at[z], z_device(peer)))
        start(remote(btop8.at[z], btop8.at[z], u_send.at[i], u_recv.at[z], z_device(peer)))
    base8[z] = bsend[:, z]
    rows = NW * docs
    every = jnp.concatenate([unpack(topics_z[at]) for at in range(nz)], axis=0)

    for at in range(nz):
        recon = dot(stack_topics(every[at * rows : (at + 1) * rows]), dsplit[z])
        data = jnp.concatenate([data32[at, owner] for owner in range(NW)], axis=0)
        high, low = split2(data / recon)
        for part, piece in enumerate((high, low, high)):
            q3[(part * nz + at) * rows : (part * nz + at + 1) * rows] = piece
    wide = turn_tall(every)
    high, low = split2(wide)
    numerator = dot(jnp.concatenate([high, high, low], axis=1), q3[...])
    new_dict = dgather[z] * numerator / jnp.sum(wide, axis=1, keepdims=True)

    onehot = (lax.broadcasted_iota(jnp.int32, (k, k), 0) == perm_in[...]).astype(F32).astype(BF16)
    aligned = dot(
        jnp.concatenate(split3(turn_flat(new_dict)), axis=1), jnp.concatenate([onehot, onehot, onehot], axis=0)
    )
    pl.semaphore_wait(line_sem.at[0], 1)
    for at in range(np_):
        p2_send[at] = pack(aligned[at * slab : (at + 1) * slab])
    for i, peer in enumerate(p_peers):
        start(remote(p2_send.at[peer], p2_recv.at[p], s_send.at[i], s_recv.at[p], p_device(peer)))
    p2_recv[p] = p2_send[p]
    for i, peer in enumerate(p_peers):
        remote(p2_send.at[peer], p2_recv.at[peer], s_send.at[i], s_recv.at[peer], p_device(peer)).wait_recv()
    median = middle([p2_recv[at] for at in range(np_)])
    p3_recv[p] = median
    for i, peer in enumerate(p_peers):
        start(remote(p3_recv.at[p], p3_recv.at[p], m_send.at[i], m_recv.at[p], p_device(peer)))
    med_ref[...] = unpack(median)
    for i, peer in enumerate(z_peers):
        remote(bsend.at[:, peer], base8.at[peer], b_send.at[i], b_recv.at[peer], z_device(peer)).wait_recv()
        remote(btop8.at[z], btop8.at[peer], u_send.at[i], u_recv.at[peer], z_device(peer)).wait_recv()
    for owner in range(NW):
        bdata[owner] = jnp.concatenate([base8[at, owner] for at in range(nz)], axis=0)
    topics = jnp.concatenate([btop8[at] for at in range(nz)], axis=0)
    stacked = stack_topics(topics)
    for i, peer in enumerate(p_peers):
        remote(p3_recv.at[p], p3_recv.at[peer], m_send.at[i], m_recv.at[peer], p_device(peer)).wait_recv()

    mgather[w] = turn_tall(jnp.concatenate([unpack(p3_recv[at]) for at in range(np_)], axis=0))
    partner, across = xh * NC + (NC - 1 - c), lax.rem(w + NC, NW)

    def median_copy(number, block, part, to):
        at = mgather.at[block, pl.ds(part * chunk2, chunk2), :]
        return remote(at, at, x_send.at[number, part], x_recv.at[block, part], w_device(to))

    for part in (0, 1):
        start(median_copy(0, w, part, across))
    for part in (0, 1):
        start(median_copy(1, w, part, partner))

    def add_block(at, columns, acc):
        split_block(mgather, msplit, at)
        return columns + column_term(msplit, at), acc + block_term(stacked, bdata[at], msplit, at)

    columns, acc = add_block(w, jnp.zeros((8, 2 * k), F32), jnp.zeros((topics.shape[0], 2 * k), F32))
    for part in (0, 1):
        median_copy(0, across, part, across).wait_recv()
        start(median_copy(2, across, part, partner))
    for part in (0, 1):
        median_copy(1, partner, part, partner).wait_recv()
    columns, acc = add_block(partner, columns, acc)
    columns, acc = add_block(across, columns, acc)
    far_block = lax.rem(partner + NC, NW)
    for part in (0, 1):
        median_copy(2, far_block, part, partner).wait_recv()
    columns, acc = add_block(far_block, columns, acc)
    product, col_total = exchange(bpartial, 0, z, z_peers, z_device, (e_send, e_recv), acc, columns)
    topics = topics * product / col_total
    for update in range(1, REFITS):
        stacked = stack_topics(topics)
        acc = sum(block_term(stacked, bdata[at], msplit, at) for at in range(NW))
        product, _ = exchange(bpartial, update, z, z_peers, z_device, (e_send, e_recv), acc, None)
        topics = topics * product / col_total
    own = topics[0:bdocs]
    for at in range(1, nz):
        own = jnp.where(z == at, topics[at * bdocs : (at + 1) * bdocs], own)
    refit_ref[...] = own

    for copy in sends:
        copy.wait_send()


def per_device(counts, tile_mask, member_topics, start_dict, align_perm, base_counts, base_topics, *, np_, nz):
    docs, bdocs = counts.shape[1], base_counts.shape[0]
    wb, k = start_dict.shape[1:]
    slab = wb // np_
    last = nz // 2
    rows, brows = NW * docs, nz * bdocs
    sem = pltpu.SemaphoreType.DMA
    scratch = [
        pltpu.VMEM(counts.shape[1:], counts.dtype),
        pltpu.VMEM(tile_mask.shape[1:], tile_mask.dtype),
        pltpu.VMEM(align_perm.shape, align_perm.dtype),
        pltpu.VMEM(base_counts.shape, base_counts.dtype),
        pltpu.VMEM((NW, nz, docs, wb), F32),
        pltpu.VMEM((NW, nz, docs, wb), F32),
        pltpu.VMEM((nz, NW, docs, wb), F32),
        pltpu.VMEM((NW, nz, bdocs, wb), F32),
        pltpu.VMEM((nz, NW, bdocs, wb), F32),
        pltpu.VMEM((NW, brows, wb), F32),
        pltpu.VMEM((NW, docs, k), F32),
        pltpu.VMEM((nz, bdocs, k), F32),
        pltpu.VMEM((nz, k, wb), F32),
        pltpu.VMEM((NW, k, wb), F32),
        pltpu.VMEM((nz, 3 * k, wb), BF16),
        pltpu.VMEM((NW, 3 * k, wb), BF16),
        pltpu.VMEM((UPDATES, NW, rows // 2 + 8, 2 * k), F32),
        pltpu.VMEM((REFITS, nz, brows // 2 + 8, 2 * k), F32),
        pltpu.VMEM((nz, rows // 2, 2 * k), F32),
        pltpu.VMEM((3 * nz * rows, wb), BF16),
        pltpu.VMEM((np_, slab // 2, 2 * k), F32),
        pltpu.VMEM((np_, slab // 2, 2 * k), F32),
        pltpu.VMEM((np_, slab // 2, 2 * k), F32),
        sem((7,)),
        pltpu.SemaphoreType.REGULAR((2, np_ // NX // 2 - 1)),
        pltpu.SemaphoreType.REGULAR((1,)),
    ]
    for _ in range(2):
        scratch += [sem((NW - 1,)), sem((NW,))]
    scratch += [sem((3, 2)), sem((NW, 2))]
    scratch += [sem((UPDATES, NW - 1)), sem((UPDATES, NW))]
    scratch += [sem((2, last, 4)), sem((2, last, 4))]
    for _ in range(4):
        scratch += [sem((nz - 1,)), sem((nz,))]
    scratch += [sem((REFITS, nz - 1)), sem((REFITS, nz))]
    for _ in range(2):
        scratch += [sem((np_ - 1,)), sem((np_,))]
    here = pl.BlockSpec(memory_space=pl.ANY)
    vmem = pl.BlockSpec(memory_space=pltpu.VMEM)
    median, refit = pl.pallas_call(
        functools.partial(kernel, np_=np_, nz=nz),
        out_shape=(jax.ShapeDtypeStruct((slab, k), F32), jax.ShapeDtypeStruct((bdocs, k), F32)),
        in_specs=[here] * 7,
        out_specs=(vmem, vmem),
        scratch_shapes=scratch,
        compiler_params=pltpu.CompilerParams(collective_id=0, has_side_effects=True),
    )(counts[0], tile_mask[0], member_topics[0], start_dict[0].T, align_perm, base_counts, base_topics)
    return median[None, None], refit


def solution(mesh):
    np_ = mesh.shape["pert"]
    nz = mesh.shape["doc"] // NW
    return jax.shard_map(
        functools.partial(per_device, np_=np_, nz=nz),
        mesh=mesh,
        in_specs=(
            P("pert", "doc", None),
            P("pert", "doc", None),
            P("pert", "doc", None),
            P("pert", "doc", None),
            P("pert", None),
            P(("pert", "doc"), None),
            P(("pert", "doc"), None),
        ),
        out_specs=(P("doc", "pert", None, None), P(("pert", "doc"), None)),
        check_vma=False,
    )
```

```python
import functools

import jax
import jax.numpy as jnp
from jax import lax
from jax.experimental import pallas as pl
from jax.experimental.pallas import tpu as pltpu
from jax.sharding import PartitionSpec as P

UPDATES = 3
REFITS = 2
NX = 2
NC = 2
NW = NX * NC
MESH = pl.DeviceIdType.MESH
F32 = jnp.float32
BF16 = jnp.bfloat16


def sort_pairs(count):
    pairs = []
    span = 1
    while span < count:
        step = span
        while step >= 1:
            for start in range(step % span, count - step, 2 * step):
                for at in range(min(step, count - start - step)):
                    low, high = start + at, start + at + step
                    if low // (2 * span) == high // (2 * span):
                        pairs.append((low, high))
            step //= 2
        span *= 2
    return pairs


def middle(rows):
    rows = list(rows)
    for low, high in sort_pairs(len(rows)):
        rows[low], rows[high] = jnp.minimum(rows[low], rows[high]), jnp.maximum(rows[low], rows[high])
    at = len(rows) // 2
    return 0.5 * (rows[at - 1] + rows[at])


def split2(x):
    high = x.astype(BF16)
    return high, (x - high.astype(F32)).astype(BF16)


def split3(x):
    high = x.astype(BF16)
    rest = x - high.astype(F32)
    mid = rest.astype(BF16)
    return high, mid, (rest - mid.astype(F32)).astype(BF16)


def pack(x):
    half = x.shape[0] // 2
    return jnp.concatenate([x[:half], x[half:]], axis=1)


def unpack(x):
    half = x.shape[1] // 2
    return jnp.concatenate([x[:, :half], x[:, half:]], axis=0)


def turn_tall(x):
    wide = jnp.concatenate([x, jnp.zeros_like(x)], axis=1)
    return wide.T[: x.shape[1]]


def turn_flat(x):
    tall = jnp.concatenate([x, jnp.zeros_like(x)], axis=0)
    return tall.T[:, : x.shape[0]]


def dot(a, b):
    return jnp.dot(a, b, preferred_element_type=F32)


def dot_nt(a, b):
    return lax.dot_general(a, b, (((1,), (1,)), ((), ())), preferred_element_type=F32)


def kernel(
    counts_ref, mask_ref, mtop_ref, dict_ref, perm_ref, base_ref, btop_ref,
    med_ref, refit_ref,
    counts_in, mask_in, perm_in, base_in,
    masked, data4, data32, bsend, base8, bdata, mtop4, btop8, dgather, mgather, dsplit, msplit,
    mpartial, bpartial, topics_z, q3, p2_send, p2_recv, p3_recv, in_sem, here_sem, line_sem, fsend, frecv, f_send, f_recv,
    w_send, w_recv, t_send, t_recv, x_send, x_recv, a_send, a_recv, r_send, r_recv,
    z_send, z_recv, g_send, g_recv, b_send, b_recv, u_send, u_recv, e_send, e_recv, s_send, s_recv, m_send, m_recv,
    *, np_, nz,
):
    k, wb = dict_ref.shape
    docs, bdocs = mtop_ref.shape[0], btop_ref.shape[0]
    p = lax.axis_index("pert")
    b = lax.axis_index("doc")
    xh, z, c = b // (nz * NC), (b // NC) % nz, b % NC
    w = xh * NC + c
    chunk, chunk2 = k // 4, k // 2
    slab = wb // np_

    def w_device(at):
        return (p, (at // NC) * (nz * NC) + z * NC + at % NC)

    def z_device(at):
        return (p, xh * (nz * NC) + at * NC + c)

    def p_device(at):
        return (at, b)

    w_peers = [lax.rem(w + i, NW) for i in range(1, NW)]
    z_peers = [lax.rem(z + i, nz) for i in range(1, nz)]
    p_peers = [lax.rem(p + i, np_) for i in range(1, np_)]

    loads = [
        pltpu.make_async_copy(src, dst, in_sem.at[i])
        for i, (src, dst) in enumerate(
            (
                (dict_ref, dgather.at[z]),
                (mask_ref, mask_in),
                (counts_ref, counts_in),
                (base_ref, base_in),
                (mtop_ref, mtop4.at[w]),
                (btop_ref, btop8.at[z]),
                (perm_ref, perm_in),
            )
        )
    ]
    for load in loads:
        load.start()

    barrier = pltpu.get_barrier_semaphore()
    ny = np_ // NX
    xl, y = p // ny, p % ny
    y_next = [p_device(xl * ny + lax.rem(y + step, ny)) for step in (1, ny - 1)]
    x_across = p_device((NX - 1 - xl) * ny + y)
    near = [w_device(peer) for peer in w_peers] + [z_device(z_peers[0]), z_device(z_peers[-1])] + y_next + [x_across]
    for device in near:
        pl.semaphore_signal(barrier, inc=1, device_id=device, device_id_type=MESH)

    loads[0].wait()
    pl.semaphore_wait(barrier, len(near))

    def tell(stage):
        if stage > 0:
            for way in (0, 1):
                pl.semaphore_wait(here_sem.at[way, stage - 1], 1)
        if stage < ny // 2 - 1:
            for way in (0, 1):
                pl.semaphore_signal(here_sem.at[way, stage], inc=1, device_id=y_next[way], device_id_type=MESH)
        else:
            pl.semaphore_signal(line_sem.at[0], inc=1, device_id=x_across, device_id_type=MESH)

    tell(0)

    sends = []

    def remote(src, dst, ssem, rsem, device):
        return pltpu.make_async_remote_copy(
            src_ref=src, dst_ref=dst, send_sem=ssem, recv_sem=rsem, device_id=device, device_id_type=MESH
        )

    def start(copy):
        copy.start()
        sends.append(copy)

    last = nz // 2

    def ring_block(way, far):
        return lax.rem(z + nz - far, nz) if way == 0 else lax.rem(z + far, nz)

    def ring_copy(way, far, ch, hops):
        at = dgather.at[ring_block(way, far), pl.ds(ch * chunk, chunk), :]
        number = far + hops - 1
        return remote(
            at, at, r_send.at[way, number, ch], r_recv.at[way, number, ch], z_device(ring_block(1 - way, hops))
        )

    def ring_first():
        for ch in range(4):
            for way in (0, 1):
                start(ring_copy(way, 0, ch, 1))

    def ring_step(far):
        for ch in range(4):
            for way in (0, 1):
                if far == last and ch // 2 != way:
                    continue
                here = dgather.at[ring_block(way, far), pl.ds(ch * chunk, chunk), :]
                remote(
                    here, here, r_send.at[way, far - 1, ch], r_recv.at[way, far - 1, ch], z_device(ring_block(1 - way, 1))
                ).wait_recv()
                if far < last - 1:
                    start(ring_copy(way, far, ch, 1))
            if far == last - 2:
                start(ring_copy(ch // 2, far, ch, 2))

    def blocks_at(far):
        if far == 0 or far == last:
            return [ring_block(0, far)]
        return [ring_block(0, far), ring_block(1, far)]

    def split_block(buf, out, at):
        high, low = split2(buf[at])
        out[at, 0:k] = high
        out[at, k : 2 * k] = low
        out[at, 2 * k : 3 * k] = high

    def stack_topics(topics):
        high, low = split2(topics)
        return jnp.concatenate([high, high, low], axis=1)

    def rows_of(at):
        return jnp.concatenate([data4[owner, at] for owner in range(NW)], axis=0)

    def block_term(stacked, data, split, at):
        rows = data.shape[0]
        high, low = split2(data / dot(stacked, split[at]))
        both = dot_nt(jnp.concatenate([high, low], axis=0), split[at, 0 : 2 * k])
        return both[:rows] + both[rows:]

    def column_term(split, at):
        return dot_nt(jnp.ones((16, wb), BF16), split[at, 0 : 2 * k])[:8]

    def fold(x):
        return x[:, :k] + x[:, k:]

    def exchange(partial, at, me, peers, device, sems, acc, columns, meanwhile=None):
        rows = acc.shape[0] // 2
        partial[at, me, 0:rows] = pack(fold(acc))
        sent = rows
        if columns is not None:
            partial[at, me, rows : rows + 8] = columns
            sent = rows + 8
        ssem, rsem = sems
        for i, peer in enumerate(peers):
            mine = partial.at[at, me, 0:sent]
            start(remote(mine, mine, ssem.at[at, i], rsem.at[at, me], device(peer)))
        if meanwhile is not None:
            meanwhile()
        for i, peer in enumerate(peers):
            theirs = partial.at[at, peer, 0:sent]
            remote(theirs, theirs, ssem.at[at, i], rsem.at[at, peer], device(peer)).wait_recv()
        total = partial[at, 0, 0:sent]
        for owner in range(1, len(peers) + 1):
            total = total + partial[at, owner, 0:sent]
        product = unpack(total[:rows])
        return product, (fold(total[rows : rows + 1]) if columns is not None else None)

    ring_first()
    for load in loads[1:]:
        load.wait()
    tiles = mask_ref.shape[1]
    tile_width = counts_ref.shape[1] // tiles
    per_block = wb // tile_width
    tile_ids = lax.broadcasted_iota(jnp.int32, (docs, tiles), 1)
    doc_ids = b * docs + lax.broadcasted_iota(jnp.int32, (docs, tiles), 0)
    occupied = jnp.maximum(mask_in[...], (tile_ids == doc_ids % tiles).astype(jnp.int32)).astype(F32)

    for owner in range(NW):

        def mask_block(zb, carry, owner=owner):
            block = ((owner // NC) * nz + zb) * NC + owner % NC
            for j in range(per_block):
                tile = block * per_block + j
                seen = jnp.sum(jnp.where(tile_ids == tile, occupied, 0.0), axis=1, keepdims=True)
                at = pl.multiple_of(tile * tile_width, tile_width)
                masked[owner, zb, :, j * tile_width : (j + 1) * tile_width] = (
                    counts_in[:, pl.ds(at, tile_width)].astype(F32) * seen
                )
            at = pl.multiple_of(block * wb, wb)
            bsend[owner, zb] = base_in[:, pl.ds(at, wb)].astype(F32)
            return carry

        lax.fori_loop(0, nz, mask_block, 0)
    for i, peer in enumerate(w_peers):
        start(remote(masked.at[peer], data4.at[w], w_send.at[i], w_recv.at[w], w_device(peer)))
        start(remote(mtop4.at[w], mtop4.at[w], t_send.at[i], t_recv.at[w], w_device(peer)))
    for far in range(1, last - 1):
        ring_step(far)
    data4[w] = masked[w]
    columns = jnp.zeros((8, 2 * k), F32)
    for far in range(last - 1):
        for at in blocks_at(far):
            split_block(dgather, dsplit, at)
            columns = columns + column_term(dsplit, at)

    for i, peer in enumerate(w_peers):
        remote(mtop4.at[w], mtop4.at[peer], t_send.at[i], t_recv.at[peer], w_device(peer)).wait_recv()
        remote(masked.at[peer], data4.at[peer], w_send.at[i], w_recv.at[peer], w_device(peer)).wait_recv()
    topics = jnp.concatenate([mtop4[owner] for owner in range(NW)], axis=0)
    stacked = stack_topics(topics)
    acc = jnp.zeros((topics.shape[0], 2 * k), F32)
    for far in range(last - 1):
        for at in blocks_at(far):
            acc = acc + block_term(stacked, rows_of(at), dsplit, at)
    for far in range(last - 1, last + 1):
        ring_step(far)
        for at in blocks_at(far):
            split_block(dgather, dsplit, at)
            columns = columns + column_term(dsplit, at)
            acc = acc + block_term(stacked, rows_of(at), dsplit, at)

    def own_words():
        for i, peer in enumerate(z_peers):
            start(remote(data4.at[:, peer], data32.at[z], z_send.at[i], z_recv.at[z], z_device(peer)))
        data32[z] = data4[:, z]
        tell(1)

    product, col_total = exchange(mpartial, 0, w, w_peers, w_device, (a_send, a_recv), acc, columns, own_words)
    topics = topics * product / col_total
    for update in range(1, UPDATES):
        stacked = stack_topics(topics)
        acc = sum(block_term(stacked, rows_of(at), dsplit, at) for at in range(nz))
        product, _ = exchange(
            mpartial, update, w, w_peers, w_device, (a_send, a_recv), acc, None, functools.partial(tell, update + 1)
        )
        topics = topics * product / col_total

    topics_z[z] = pack(topics)
    for i, peer in enumerate(z_peers):
        start(remote(topics_z.at[z], topics_z.at[z], g_send.at[i], g_recv.at[z], z_device(peer)))
    rows = NW * docs

    def add_quotient(at):
        recon = dot(stack_topics(unpack(topics_z[at])), dsplit[z])
        data = jnp.concatenate([data32[at, owner] for owner in range(NW)], axis=0)
        high, low = split2(data / recon)
        for part, piece in enumerate((high, low, high)):
            q3[pl.ds(pl.multiple_of((part * nz + at) * rows, rows), rows)] = piece

    add_quotient(z)
    order = [i for far in range(nz // 2) for i in sorted({far, nz - 2 - far})]
    for i in order:
        peer = z_peers[i]
        remote(data4.at[:, peer], data32.at[peer], z_send.at[i], z_recv.at[peer], z_device(peer)).wait_recv()
        remote(topics_z.at[z], topics_z.at[peer], g_send.at[i], g_recv.at[peer], z_device(peer)).wait_recv()
        add_quotient(peer)
    every = jnp.concatenate([unpack(topics_z[at]) for at in range(nz)], axis=0)
    wide = turn_tall(every)
    high, low = split2(wide)
    numerator = dot(jnp.concatenate([high, high, low], axis=1), q3[...])
    new_dict = dgather[z] * numerator / jnp.sum(wide, axis=1, keepdims=True)

    onehot = (lax.broadcasted_iota(jnp.int32, (k, k), 0) == perm_in[...]).astype(F32).astype(BF16)
    aligned = dot(
        jnp.concatenate(split3(turn_flat(new_dict)), axis=1), jnp.concatenate([onehot, onehot, onehot], axis=0)
    )
    pl.semaphore_wait(line_sem.at[0], 1)
    for at in range(np_):
        p2_send[at] = pack(aligned[at * slab : (at + 1) * slab])
    for i, peer in enumerate(p_peers):
        start(remote(p2_send.at[peer], p2_recv.at[p], s_send.at[i], s_recv.at[p], p_device(peer)))
    p2_recv[p] = p2_send[p]
    for i, peer in enumerate(z_peers):
        start(remote(bsend.at[:, peer], base8.at[z], b_send.at[i], b_recv.at[z], z_device(peer)))
        start(remote(btop8.at[z], btop8.at[z], u_send.at[i], u_recv.at[z], z_device(peer)))
    base8[z] = bsend[:, z]
    for i, peer in enumerate(p_peers):
        remote(p2_send.at[peer], p2_recv.at[peer], s_send.at[i], s_recv.at[peer], p_device(peer)).wait_recv()
    median = middle([p2_recv[at] for at in range(np_)])
    p3_recv[p] = median
    for i, peer in enumerate(p_peers):
        start(remote(p3_recv.at[p], p3_recv.at[p], m_send.at[i], m_recv.at[p], p_device(peer)))
    med_ref[...] = unpack(median)
    for i, peer in enumerate(p_peers):
        remote(p3_recv.at[p], p3_recv.at[peer], m_send.at[i], m_recv.at[peer], p_device(peer)).wait_recv()

    mgather[w] = turn_tall(jnp.concatenate([unpack(p3_recv[at]) for at in range(np_)], axis=0))
    partner, across = xh * NC + (NC - 1 - c), lax.rem(w + NC, NW)

    def median_copy(number, block, part, to):
        at = mgather.at[block, pl.ds(part * chunk2, chunk2), :]
        return remote(at, at, x_send.at[number, part], x_recv.at[block, part], w_device(to))

    for part in (0, 1):
        start(median_copy(0, w, part, across))
    for part in (0, 1):
        start(median_copy(1, w, part, partner))
    for i, peer in enumerate(z_peers):
        remote(bsend.at[:, peer], base8.at[peer], b_send.at[i], b_recv.at[peer], z_device(peer)).wait_recv()
        remote(btop8.at[z], btop8.at[peer], u_send.at[i], u_recv.at[peer], z_device(peer)).wait_recv()
    for owner in range(NW):
        bdata[owner] = jnp.concatenate([base8[at, owner] for at in range(nz)], axis=0)
    topics = jnp.concatenate([btop8[at] for at in range(nz)], axis=0)
    stacked = stack_topics(topics)

    def add_block(at, columns, acc):
        split_block(mgather, msplit, at)
        return columns + column_term(msplit, at), acc + block_term(stacked, bdata[at], msplit, at)

    columns, acc = add_block(w, jnp.zeros((8, 2 * k), F32), jnp.zeros((topics.shape[0], 2 * k), F32))
    for part in (0, 1):
        median_copy(1, partner, part, partner).wait_recv()
    columns, acc = add_block(partner, columns, acc)
    for part in (0, 1):
        median_copy(0, across, part, across).wait_recv()
        start(median_copy(2, across, part, partner))
    columns, acc = add_block(across, columns, acc)
    far_block = lax.rem(partner + NC, NW)
    for part in (0, 1):
        median_copy(2, far_block, part, partner).wait_recv()
    columns, acc = add_block(far_block, columns, acc)
    product, col_total = exchange(bpartial, 0, z, z_peers, z_device, (e_send, e_recv), acc, columns)
    topics = topics * product / col_total
    for update in range(1, REFITS - 1):
        stacked = stack_topics(topics)
        acc = sum(block_term(stacked, bdata[at], msplit, at) for at in range(NW))
        product, _ = exchange(bpartial, update, z, z_peers, z_device, (e_send, e_recv), acc, None)
        topics = topics * product / col_total
    stacked = stack_topics(topics)
    part = fold(sum(block_term(stacked, bdata[at], msplit, at) for at in range(NW)))
    for at in range(nz):
        fsend[at] = part[at * bdocs : (at + 1) * bdocs]
    for i, peer in enumerate(z_peers):
        start(remote(fsend.at[peer], frecv.at[z], f_send.at[i], f_recv.at[z], z_device(peer)))
    frecv[z] = fsend[z]
    own = topics[0:bdocs]
    for at in range(1, nz):
        own = jnp.where(z == at, topics[at * bdocs : (at + 1) * bdocs], own)
    for i, peer in enumerate(z_peers):
        remote(fsend.at[peer], frecv.at[peer], f_send.at[i], f_recv.at[peer], z_device(peer)).wait_recv()
    product = frecv[0]
    for at in range(1, nz):
        product = product + frecv[at]
    refit_ref[...] = own * product / col_total

    for copy in sends:
        copy.wait_send()


def per_device(counts, tile_mask, member_topics, start_dict, align_perm, base_counts, base_topics, *, np_, nz):
    docs, bdocs = counts.shape[1], base_counts.shape[0]
    wb, k = start_dict.shape[1:]
    slab = wb // np_
    last = nz // 2
    rows, brows = NW * docs, nz * bdocs
    sem = pltpu.SemaphoreType.DMA
    scratch = [
        pltpu.VMEM(counts.shape[1:], counts.dtype),
        pltpu.VMEM(tile_mask.shape[1:], tile_mask.dtype),
        pltpu.VMEM(align_perm.shape, align_perm.dtype),
        pltpu.VMEM(base_counts.shape, base_counts.dtype),
        pltpu.VMEM((NW, nz, docs, wb), F32),
        pltpu.VMEM((NW, nz, docs, wb), F32),
        pltpu.VMEM((nz, NW, docs, wb), F32),
        pltpu.VMEM((NW, nz, bdocs, wb), F32),
        pltpu.VMEM((nz, NW, bdocs, wb), F32),
        pltpu.VMEM((NW, brows, wb), F32),
        pltpu.VMEM((NW, docs, k), F32),
        pltpu.VMEM((nz, bdocs, k), F32),
        pltpu.VMEM((nz, k, wb), F32),
        pltpu.VMEM((NW, k, wb), F32),
        pltpu.VMEM((nz, 3 * k, wb), BF16),
        pltpu.VMEM((NW, 3 * k, wb), BF16),
        pltpu.VMEM((UPDATES, NW, rows // 2 + 8, 2 * k), F32),
        pltpu.VMEM((REFITS, nz, brows // 2 + 8, 2 * k), F32),
        pltpu.VMEM((nz, rows // 2, 2 * k), F32),
        pltpu.VMEM((3 * nz * rows, wb), BF16),
        pltpu.VMEM((np_, slab // 2, 2 * k), F32),
        pltpu.VMEM((np_, slab // 2, 2 * k), F32),
        pltpu.VMEM((np_, slab // 2, 2 * k), F32),
        sem((7,)),
        pltpu.SemaphoreType.REGULAR((2, np_ // NX // 2 - 1)),
        pltpu.SemaphoreType.REGULAR((1,)),
        pltpu.VMEM((nz, bdocs, k), F32),
        pltpu.VMEM((nz, bdocs, k), F32),
        sem((nz - 1,)),
        sem((nz,)),
    ]
    for _ in range(2):
        scratch += [sem((NW - 1,)), sem((NW,))]
    scratch += [sem((3, 2)), sem((NW, 2))]
    scratch += [sem((UPDATES, NW - 1)), sem((UPDATES, NW))]
    scratch += [sem((2, last, 4)), sem((2, last, 4))]
    for _ in range(4):
        scratch += [sem((nz - 1,)), sem((nz,))]
    scratch += [sem((REFITS, nz - 1)), sem((REFITS, nz))]
    for _ in range(2):
        scratch += [sem((np_ - 1,)), sem((np_,))]
    here = pl.BlockSpec(memory_space=pl.ANY)
    vmem = pl.BlockSpec(memory_space=pltpu.VMEM)
    median, refit = pl.pallas_call(
        functools.partial(kernel, np_=np_, nz=nz),
        out_shape=(jax.ShapeDtypeStruct((slab, k), F32), jax.ShapeDtypeStruct((bdocs, k), F32)),
        in_specs=[here] * 7,
        out_specs=(vmem, vmem),
        scratch_shapes=scratch,
        compiler_params=pltpu.CompilerParams(collective_id=0, has_side_effects=True),
    )(counts[0], tile_mask[0], member_topics[0], start_dict[0].T, align_perm, base_counts, base_topics)
    return median[None, None], refit


def solution(mesh):
    np_ = mesh.shape["pert"]
    nz = mesh.shape["doc"] // NW
    return jax.shard_map(
        functools.partial(per_device, np_=np_, nz=nz),
        mesh=mesh,
        in_specs=(
            P("pert", "doc", None),
            P("pert", "doc", None),
            P("pert", "doc", None),
            P("pert", "doc", None),
            P("pert", None),
            P(("pert", "doc"), None),
            P(("pert", "doc"), None),
        ),
        out_specs=(P("doc", "pert", None, None), P(("pert", "doc"), None)),
        check_vma=False,
    )
```

```python
import functools

import jax
import jax.numpy as jnp
from jax import lax
from jax.experimental import pallas as pl
from jax.experimental.pallas import tpu as pltpu
from jax.sharding import PartitionSpec as P

UPDATES = 3
REFITS = 2
NX = 2
NC = 2
NW = NX * NC
MESH = pl.DeviceIdType.MESH
F32 = jnp.float32
BF16 = jnp.bfloat16


def sort_pairs(count):
    pairs = []
    span = 1
    while span < count:
        step = span
        while step >= 1:
            for start in range(step % span, count - step, 2 * step):
                for at in range(min(step, count - start - step)):
                    low, high = start + at, start + at + step
                    if low // (2 * span) == high // (2 * span):
                        pairs.append((low, high))
            step //= 2
        span *= 2
    return pairs


def middle(rows):
    rows = list(rows)
    for low, high in sort_pairs(len(rows)):
        rows[low], rows[high] = jnp.minimum(rows[low], rows[high]), jnp.maximum(rows[low], rows[high])
    at = len(rows) // 2
    return 0.5 * (rows[at - 1] + rows[at])


def split2(x):
    high = x.astype(BF16)
    return high, (x - high.astype(F32)).astype(BF16)


def split3(x):
    high = x.astype(BF16)
    rest = x - high.astype(F32)
    mid = rest.astype(BF16)
    return high, mid, (rest - mid.astype(F32)).astype(BF16)


def pack(x):
    half = x.shape[0] // 2
    return jnp.concatenate([x[:half], x[half:]], axis=1)


def unpack(x):
    half = x.shape[1] // 2
    return jnp.concatenate([x[:, :half], x[:, half:]], axis=0)


def turn_tall(x):
    wide = jnp.concatenate([x, jnp.zeros_like(x)], axis=1)
    return wide.T[: x.shape[1]]


def turn_flat(x):
    tall = jnp.concatenate([x, jnp.zeros_like(x)], axis=0)
    return tall.T[:, : x.shape[0]]


def dot(a, b):
    return jnp.dot(a, b, preferred_element_type=F32)


def dot_nt(a, b):
    return lax.dot_general(a, b, (((1,), (1,)), ((), ())), preferred_element_type=F32)


def kernel(
    counts_ref, mask_ref, mtop_ref, dict_ref, perm_ref, base_ref, btop_ref,
    med_ref, refit_ref,
    counts_in, mask_in, perm_in, base_in,
    masked, data4, data32, bsend, base8, bdata, mtop4, btop8, dgather, mgather, dsplit, msplit,
    mpartial, bpartial, topics_z, q3, p2_send, p2_recv, p3_recv, in_sem, here_sem, line_sem, fsend, frecv, f_send, f_recv,
    w_send, w_recv, t_send, t_recv, x_send, x_recv, a_send, a_recv, r_send, r_recv,
    z_send, z_recv, g_send, g_recv, b_send, b_recv, u_send, u_recv, e_send, e_recv, s_send, s_recv, m_send, m_recv,
    *, np_, nz,
):
    k, wb = dict_ref.shape
    docs, bdocs = mtop_ref.shape[0], btop_ref.shape[0]
    p = lax.axis_index("pert")
    b = lax.axis_index("doc")
    xh, z, c = b // (nz * NC), (b // NC) % nz, b % NC
    w = xh * NC + c
    chunk, chunk2 = k // 4, k // 2
    slab = wb // np_

    def w_device(at):
        return (p, (at // NC) * (nz * NC) + z * NC + at % NC)

    def z_device(at):
        return (p, xh * (nz * NC) + at * NC + c)

    def p_device(at):
        return (at, b)

    w_peers = [lax.rem(w + i, NW) for i in range(1, NW)]
    z_peers = [lax.rem(z + i, nz) for i in range(1, nz)]
    p_steps = sorted(range(1, np_), key=lambda i: -min(i % (np_ // NX), -i % (np_ // NX)))
    p_peers = [lax.rem(p + i, np_) for i in p_steps]
    z_far = sorted(enumerate(z_peers), key=lambda pair: abs(pair[0] + 1 - nz // 2))

    loads = [
        pltpu.make_async_copy(src, dst, in_sem.at[i])
        for i, (src, dst) in enumerate(
            (
                (dict_ref, dgather.at[z]),
                (mask_ref, mask_in),
                (counts_ref, counts_in),
                (base_ref, base_in),
                (mtop_ref, mtop4.at[w]),
                (btop_ref, btop8.at[z]),
                (perm_ref, perm_in),
            )
        )
    ]
    for load in loads:
        load.start()

    barrier = pltpu.get_barrier_semaphore()
    ny = np_ // NX
    xl, y = p // ny, p % ny
    y_next = [p_device(xl * ny + lax.rem(y + step, ny)) for step in (1, ny - 1)]
    x_across = p_device((NX - 1 - xl) * ny + y)
    near = [w_device(peer) for peer in w_peers] + [z_device(z_peers[0]), z_device(z_peers[-1])] + y_next + [x_across]
    for device in near:
        pl.semaphore_signal(barrier, inc=1, device_id=device, device_id_type=MESH)

    loads[0].wait()
    pl.semaphore_wait(barrier, len(near))

    def tell(stage):
        if stage > 0:
            for way in (0, 1):
                pl.semaphore_wait(here_sem.at[way, stage - 1], 1)
        if stage < ny // 2 - 1:
            for way in (0, 1):
                pl.semaphore_signal(here_sem.at[way, stage], inc=1, device_id=y_next[way], device_id_type=MESH)
        else:
            pl.semaphore_signal(line_sem.at[0], inc=1, device_id=x_across, device_id_type=MESH)

    tell(0)

    sends = []

    def remote(src, dst, ssem, rsem, device):
        return pltpu.make_async_remote_copy(
            src_ref=src, dst_ref=dst, send_sem=ssem, recv_sem=rsem, device_id=device, device_id_type=MESH
        )

    def start(copy):
        copy.start()
        sends.append(copy)

    last = nz // 2

    def ring_block(way, far):
        return lax.rem(z + nz - far, nz) if way == 0 else lax.rem(z + far, nz)

    def ring_copy(way, far, ch, hops):
        at = dgather.at[ring_block(way, far), pl.ds(ch * chunk, chunk), :]
        number = far + hops - 1
        return remote(
            at, at, r_send.at[way, number, ch], r_recv.at[way, number, ch], z_device(ring_block(1 - way, hops))
        )

    def ring_first():
        for ch in range(4):
            for way in (0, 1):
                start(ring_copy(way, 0, ch, 1))

    def ring_step(far):
        for ch in range(4):
            for way in (0, 1):
                if far == last and ch // 2 != way:
                    continue
                here = dgather.at[ring_block(way, far), pl.ds(ch * chunk, chunk), :]
                remote(
                    here, here, r_send.at[way, far - 1, ch], r_recv.at[way, far - 1, ch], z_device(ring_block(1 - way, 1))
                ).wait_recv()
                if far < last - 1:
                    start(ring_copy(way, far, ch, 1))
            if far == last - 2:
                start(ring_copy(ch // 2, far, ch, 2))

    def blocks_at(far):
        if far == 0 or far == last:
            return [ring_block(0, far)]
        return [ring_block(0, far), ring_block(1, far)]

    def split_block(buf, out, at):
        high, low = split2(buf[at])
        out[at, 0:k] = high
        out[at, k : 2 * k] = low
        out[at, 2 * k : 3 * k] = high

    def stack_topics(topics):
        high, low = split2(topics)
        return jnp.concatenate([high, high, low], axis=1)

    def rows_of(at):
        return jnp.concatenate([data4[owner, at] for owner in range(NW)], axis=0)

    def block_term(stacked, data, split, at):
        rows = data.shape[0]
        high, low = split2(data / dot(stacked, split[at]))
        both = dot_nt(jnp.concatenate([high, low], axis=0), split[at, 0 : 2 * k])
        return both[:rows] + both[rows:]

    def column_term(split, at):
        return dot_nt(jnp.ones((16, wb), BF16), split[at, 0 : 2 * k])[:8]

    def fold(x):
        return x[:, :k] + x[:, k:]

    def exchange(partial, at, me, peers, device, sems, acc, columns, meanwhile=None):
        rows = acc.shape[0] // 2
        partial[at, me, 0:rows] = pack(fold(acc))
        sent = rows
        if columns is not None:
            partial[at, me, rows : rows + 8] = columns
            sent = rows + 8
        ssem, rsem = sems
        for i, peer in enumerate(peers):
            mine = partial.at[at, me, 0:sent]
            start(remote(mine, mine, ssem.at[at, i], rsem.at[at, me], device(peer)))
        if meanwhile is not None:
            meanwhile()
        for i, peer in enumerate(peers):
            theirs = partial.at[at, peer, 0:sent]
            remote(theirs, theirs, ssem.at[at, i], rsem.at[at, peer], device(peer)).wait_recv()
        total = partial[at, 0, 0:sent]
        for owner in range(1, len(peers) + 1):
            total = total + partial[at, owner, 0:sent]
        product = unpack(total[:rows])
        return product, (fold(total[rows : rows + 1]) if columns is not None else None)

    ring_first()
    for load in loads[1:]:
        load.wait()
    tiles = mask_ref.shape[1]
    tile_width = counts_ref.shape[1] // tiles
    per_block = wb // tile_width
    tile_ids = lax.broadcasted_iota(jnp.int32, (docs, tiles), 1)
    doc_ids = b * docs + lax.broadcasted_iota(jnp.int32, (docs, tiles), 0)
    occupied = jnp.maximum(mask_in[...], (tile_ids == doc_ids % tiles).astype(jnp.int32)).astype(F32)

    for owner in range(NW):

        def mask_block(zb, carry, owner=owner):
            block = ((owner // NC) * nz + zb) * NC + owner % NC
            for j in range(per_block):
                tile = block * per_block + j
                seen = jnp.sum(jnp.where(tile_ids == tile, occupied, 0.0), axis=1, keepdims=True)
                at = pl.multiple_of(tile * tile_width, tile_width)
                masked[owner, zb, :, j * tile_width : (j + 1) * tile_width] = (
                    counts_in[:, pl.ds(at, tile_width)].astype(F32) * seen
                )
            at = pl.multiple_of(block * wb, wb)
            bsend[owner, zb] = base_in[:, pl.ds(at, wb)].astype(F32)
            return carry

        lax.fori_loop(0, nz, mask_block, 0)
    for i, peer in enumerate(w_peers):
        start(remote(masked.at[peer], data4.at[w], w_send.at[i], w_recv.at[w], w_device(peer)))
        start(remote(mtop4.at[w], mtop4.at[w], t_send.at[i], t_recv.at[w], w_device(peer)))
    for far in range(1, last - 1):
        ring_step(far)
    data4[w] = masked[w]
    columns = jnp.zeros((8, 2 * k), F32)
    for far in range(last - 1):
        for at in blocks_at(far):
            split_block(dgather, dsplit, at)
            columns = columns + column_term(dsplit, at)

    for i, peer in enumerate(w_peers):
        remote(mtop4.at[w], mtop4.at[peer], t_send.at[i], t_recv.at[peer], w_device(peer)).wait_recv()
        remote(masked.at[peer], data4.at[peer], w_send.at[i], w_recv.at[peer], w_device(peer)).wait_recv()
    topics = jnp.concatenate([mtop4[owner] for owner in range(NW)], axis=0)
    stacked = stack_topics(topics)
    acc = jnp.zeros((topics.shape[0], 2 * k), F32)
    for far in range(last - 1):
        for at in blocks_at(far):
            acc = acc + block_term(stacked, rows_of(at), dsplit, at)
    for far in range(last - 1, last + 1):
        ring_step(far)
        for at in blocks_at(far):
            split_block(dgather, dsplit, at)
            columns = columns + column_term(dsplit, at)
            acc = acc + block_term(stacked, rows_of(at), dsplit, at)

    def own_words():
        for i, peer in enumerate(z_peers):
            start(remote(data4.at[:, peer], data32.at[z], z_send.at[i], z_recv.at[z], z_device(peer)))
        data32[z] = data4[:, z]
        tell(1)

    product, col_total = exchange(mpartial, 0, w, w_peers, w_device, (a_send, a_recv), acc, columns, own_words)
    topics = topics * product / col_total
    for update in range(1, UPDATES):
        stacked = stack_topics(topics)
        acc = sum(block_term(stacked, rows_of(at), dsplit, at) for at in range(nz))
        product, _ = exchange(
            mpartial, update, w, w_peers, w_device, (a_send, a_recv), acc, None, functools.partial(tell, update + 1)
        )
        topics = topics * product / col_total

    topics_z[z] = pack(topics)
    for i, peer in z_far:
        start(remote(topics_z.at[z], topics_z.at[z], g_send.at[i], g_recv.at[z], z_device(peer)))
    rows = NW * docs

    def add_quotient(at):
        recon = dot(stack_topics(unpack(topics_z[at])), dsplit[z])
        data = jnp.concatenate([data32[at, owner] for owner in range(NW)], axis=0)
        high, low = split2(data / recon)
        for part, piece in enumerate((high, low, high)):
            q3[pl.ds(pl.multiple_of((part * nz + at) * rows, rows), rows)] = piece

    add_quotient(z)
    order = [i for far in range(nz // 2) for i in sorted({far, nz - 2 - far})]
    for i in order:
        peer = z_peers[i]
        remote(data4.at[:, peer], data32.at[peer], z_send.at[i], z_recv.at[peer], z_device(peer)).wait_recv()
        remote(topics_z.at[z], topics_z.at[peer], g_send.at[i], g_recv.at[peer], z_device(peer)).wait_recv()
        add_quotient(peer)
    every = jnp.concatenate([unpack(topics_z[at]) for at in range(nz)], axis=0)
    wide = turn_tall(every)
    high, low = split2(wide)
    numerator = dot(jnp.concatenate([high, high, low], axis=1), q3[...])
    new_dict = dgather[z] * numerator / jnp.sum(wide, axis=1, keepdims=True)

    onehot = (lax.broadcasted_iota(jnp.int32, (k, k), 0) == perm_in[...]).astype(F32).astype(BF16)
    aligned = dot(
        jnp.concatenate(split3(turn_flat(new_dict)), axis=1), jnp.concatenate([onehot, onehot, onehot], axis=0)
    )
    pl.semaphore_wait(line_sem.at[0], 1)
    for at in range(np_):
        p2_send[at] = pack(aligned[at * slab : (at + 1) * slab])
    for i, peer in enumerate(p_peers):
        start(remote(p2_send.at[peer], p2_recv.at[p], s_send.at[i], s_recv.at[p], p_device(peer)))
    p2_recv[p] = p2_send[p]
    for i, peer in enumerate(z_peers):
        start(remote(bsend.at[:, peer], base8.at[z], b_send.at[i], b_recv.at[z], z_device(peer)))
        start(remote(btop8.at[z], btop8.at[z], u_send.at[i], u_recv.at[z], z_device(peer)))
    base8[z] = bsend[:, z]
    for i, peer in enumerate(p_peers):
        remote(p2_send.at[peer], p2_recv.at[peer], s_send.at[i], s_recv.at[peer], p_device(peer)).wait_recv()
    median = middle([p2_recv[at] for at in range(np_)])
    p3_recv[p] = median
    for i, peer in enumerate(p_peers):
        start(remote(p3_recv.at[p], p3_recv.at[p], m_send.at[i], m_recv.at[p], p_device(peer)))
    med_ref[...] = unpack(median)
    for i, peer in enumerate(p_peers):
        remote(p3_recv.at[p], p3_recv.at[peer], m_send.at[i], m_recv.at[peer], p_device(peer)).wait_recv()

    mgather[w] = turn_tall(jnp.concatenate([unpack(p3_recv[at]) for at in range(np_)], axis=0))
    partner, across = xh * NC + (NC - 1 - c), lax.rem(w + NC, NW)

    def median_copy(number, block, part, to):
        at = mgather.at[block, pl.ds(part * chunk2, chunk2), :]
        return remote(at, at, x_send.at[number, part], x_recv.at[block, part], w_device(to))

    for part in (0, 1):
        start(median_copy(0, w, part, across))
    for part in (0, 1):
        start(median_copy(1, w, part, partner))
    for i, peer in enumerate(z_peers):
        remote(bsend.at[:, peer], base8.at[peer], b_send.at[i], b_recv.at[peer], z_device(peer)).wait_recv()
        remote(btop8.at[z], btop8.at[peer], u_send.at[i], u_recv.at[peer], z_device(peer)).wait_recv()
    for owner in range(NW):
        bdata[owner] = jnp.concatenate([base8[at, owner] for at in range(nz)], axis=0)
    topics = jnp.concatenate([btop8[at] for at in range(nz)], axis=0)
    stacked = stack_topics(topics)

    def add_block(at, columns, acc):
        split_block(mgather, msplit, at)
        return columns + column_term(msplit, at), acc + block_term(stacked, bdata[at], msplit, at)

    columns, acc = add_block(w, jnp.zeros((8, 2 * k), F32), jnp.zeros((topics.shape[0], 2 * k), F32))
    for part in (0, 1):
        median_copy(1, partner, part, partner).wait_recv()
    columns, acc = add_block(partner, columns, acc)
    for part in (0, 1):
        median_copy(0, across, part, across).wait_recv()
        start(median_copy(2, across, part, partner))
    columns, acc = add_block(across, columns, acc)
    far_block = lax.rem(partner + NC, NW)
    for part in (0, 1):
        median_copy(2, far_block, part, partner).wait_recv()
    columns, acc = add_block(far_block, columns, acc)
    product, col_total = exchange(bpartial, 0, z, z_peers, z_device, (e_send, e_recv), acc, columns)
    topics = topics * product / col_total
    for update in range(1, REFITS - 1):
        stacked = stack_topics(topics)
        acc = sum(block_term(stacked, bdata[at], msplit, at) for at in range(NW))
        product, _ = exchange(bpartial, update, z, z_peers, z_device, (e_send, e_recv), acc, None)
        topics = topics * product / col_total
    stacked = stack_topics(topics)
    part = fold(sum(block_term(stacked, bdata[at], msplit, at) for at in range(NW)))
    for at in range(nz):
        fsend[at] = part[at * bdocs : (at + 1) * bdocs]
    for i, peer in z_far:
        start(remote(fsend.at[peer], frecv.at[z], f_send.at[i], f_recv.at[z], z_device(peer)))
    frecv[z] = fsend[z]
    own = topics[0:bdocs]
    for at in range(1, nz):
        own = jnp.where(z == at, topics[at * bdocs : (at + 1) * bdocs], own)
    for i, peer in enumerate(z_peers):
        remote(fsend.at[peer], frecv.at[peer], f_send.at[i], f_recv.at[peer], z_device(peer)).wait_recv()
    product = frecv[0]
    for at in range(1, nz):
        product = product + frecv[at]
    refit_ref[...] = own * product / col_total

    for copy in sends:
        copy.wait_send()


def per_device(counts, tile_mask, member_topics, start_dict, align_perm, base_counts, base_topics, *, np_, nz):
    docs, bdocs = counts.shape[1], base_counts.shape[0]
    wb, k = start_dict.shape[1:]
    slab = wb // np_
    last = nz // 2
    rows, brows = NW * docs, nz * bdocs
    sem = pltpu.SemaphoreType.DMA
    scratch = [
        pltpu.VMEM(counts.shape[1:], counts.dtype),
        pltpu.VMEM(tile_mask.shape[1:], tile_mask.dtype),
        pltpu.VMEM(align_perm.shape, align_perm.dtype),
        pltpu.VMEM(base_counts.shape, base_counts.dtype),
        pltpu.VMEM((NW, nz, docs, wb), F32),
        pltpu.VMEM((NW, nz, docs, wb), F32),
        pltpu.VMEM((nz, NW, docs, wb), F32),
        pltpu.VMEM((NW, nz, bdocs, wb), F32),
        pltpu.VMEM((nz, NW, bdocs, wb), F32),
        pltpu.VMEM((NW, brows, wb), F32),
        pltpu.VMEM((NW, docs, k), F32),
        pltpu.VMEM((nz, bdocs, k), F32),
        pltpu.VMEM((nz, k, wb), F32),
        pltpu.VMEM((NW, k, wb), F32),
        pltpu.VMEM((nz, 3 * k, wb), BF16),
        pltpu.VMEM((NW, 3 * k, wb), BF16),
        pltpu.VMEM((UPDATES, NW, rows // 2 + 8, 2 * k), F32),
        pltpu.VMEM((REFITS, nz, brows // 2 + 8, 2 * k), F32),
        pltpu.VMEM((nz, rows // 2, 2 * k), F32),
        pltpu.VMEM((3 * nz * rows, wb), BF16),
        pltpu.VMEM((np_, slab // 2, 2 * k), F32),
        pltpu.VMEM((np_, slab // 2, 2 * k), F32),
        pltpu.VMEM((np_, slab // 2, 2 * k), F32),
        sem((7,)),
        pltpu.SemaphoreType.REGULAR((2, np_ // NX // 2 - 1)),
        pltpu.SemaphoreType.REGULAR((1,)),
        pltpu.VMEM((nz, bdocs, k), F32),
        pltpu.VMEM((nz, bdocs, k), F32),
        sem((nz - 1,)),
        sem((nz,)),
    ]
    for _ in range(2):
        scratch += [sem((NW - 1,)), sem((NW,))]
    scratch += [sem((3, 2)), sem((NW, 2))]
    scratch += [sem((UPDATES, NW - 1)), sem((UPDATES, NW))]
    scratch += [sem((2, last, 4)), sem((2, last, 4))]
    for _ in range(4):
        scratch += [sem((nz - 1,)), sem((nz,))]
    scratch += [sem((REFITS, nz - 1)), sem((REFITS, nz))]
    for _ in range(2):
        scratch += [sem((np_ - 1,)), sem((np_,))]
    here = pl.BlockSpec(memory_space=pl.ANY)
    vmem = pl.BlockSpec(memory_space=pltpu.VMEM)
    median, refit = pl.pallas_call(
        functools.partial(kernel, np_=np_, nz=nz),
        out_shape=(jax.ShapeDtypeStruct((slab, k), F32), jax.ShapeDtypeStruct((bdocs, k), F32)),
        in_specs=[here] * 7,
        out_specs=(vmem, vmem),
        scratch_shapes=scratch,
        compiler_params=pltpu.CompilerParams(collective_id=0, has_side_effects=True),
    )(counts[0], tile_mask[0], member_topics[0], start_dict[0].T, align_perm, base_counts, base_topics)
    return median[None, None], refit


def solution(mesh):
    np_ = mesh.shape["pert"]
    nz = mesh.shape["doc"] // NW
    return jax.shard_map(
        functools.partial(per_device, np_=np_, nz=nz),
        mesh=mesh,
        in_specs=(
            P("pert", "doc", None),
            P("pert", "doc", None),
            P("pert", "doc", None),
            P("pert", "doc", None),
            P("pert", None),
            P(("pert", "doc"), None),
            P(("pert", "doc"), None),
        ),
        out_specs=(P("doc", "pert", None, None), P(("pert", "doc"), None)),
        check_vma=False,
    )
```
